32 devices in a mesh: grp: 2 (over x), long: 16 (over z, y, core).
Axes of the slice: x: 2, y: 2, z: 4, core: 2. Of those that a mesh axis runs over, the one named last changes fastest.
Arguments:
- pixel_map: int32 [256, 2048], P(('grp', 'long')), parts along dimension 0, may hold values from 0 to 3
- materials: float32 [8], P('grp'), parts along dimension 0, may hold values from 1.5 to 12
- mode_panel: float32 [128, 2, 201, 201], P(('grp', 'long')), parts along dimension 0, may hold values from -1.6 to 1.6
Outputs:
- coupled_panel: float32 [128, 2, 201, 201], P(('grp', 'long')), parts along dimension 0
The draws below stay inside these ranges and needn't reach their ends.
There are 2 independent parts, one for each index of `grp`. The reference program is written for one: setup_inputs(seed, part) draws one part's arguments, and reference() takes and returns one part's arrays. A program takes and returns all parts, laid end to end along the dimension named above; each array names one. Nothing has to cross between parts.
All inputs are finite; a program needn't handle non-finite values.
Results may differ from the reference program's by a relative error of at most 0.0003.
Values sent between devices are 32-bit elements; how exact they have to be, the bound alone decides.
No kernel may reach another device: no remote copies, remote signals or barrier semaphores. Data moves between devices by JAX's collectives and lax.ppermute only.
A program may use at most 128 MiB of HBM per device.

```python
import math
import jax
import jax.numpy as jnp
from jax import lax

NPIX = 2048
ORD = 201
YORD = 201
COLS = 64
NMAT = 4
NS_ITERS = 3
LINES = 128


def draw_pixel_map(key, part):
    first_key, second_key = jax.random.split(jax.random.fold_in(key, 11))
    edges = jax.random.randint(first_key, (LINES, NPIX), 0, 16)
    starts = (edges == 0).astype(jnp.int32)
    segment = jnp.cumsum(starts, axis=1).astype(jnp.int32)
    labels = jax.random.randint(second_key, (LINES, NPIX + 1), 0, NMAT)
    return jnp.take_along_axis(labels, segment, axis=1).astype(jnp.int32)


def steps_of(stream_key, shape, pieces, low, high):
    def one(position, parts):
        steps = jax.random.uniform(jax.random.fold_in(jax.random.fold_in(stream_key, 6), position), (parts,), jnp.float32, low / len(pieces), high / len(pieces))
        return jnp.repeat(jnp.exp(steps), shape[position] // parts).reshape((-1,) + (1,) * (len(shape) - position - 1))

    loudness = one(*pieces[0])
    for cut in pieces[1:]:
        loudness = loudness * one(*cut)
    return loudness


def scatter_about(stream_key, dims, spread, limit, cuts=(), kind=jnp.bfloat16):
    result = jax.random.normal(stream_key, dims, jnp.float32) * spread
    if len(cuts) > 0:
        result = steps_of(stream_key, dims, cuts, -0.22, 0.18) * result
    return jnp.clip(result, min=-limit, max=limit).astype(kind)


def setup_inputs(seed: int = 0, part: int = 0) -> dict:
    keys = jax.random.split(jax.random.key(seed), 4)
    own_keys = jax.random.split(jax.random.fold_in(keys[3], part), 4)
    pixel_map = draw_pixel_map(jax.random.fold_in(jax.random.fold_in(keys[3], part), 71), part)
    materials = jnp.clip(jax.random.uniform(own_keys[1], (NMAT,), jnp.float32, 1.5, 12.0), 1.5, 12.0)
    mode_panel = scatter_about(own_keys[2], (COLS, 2, YORD, ORD), 0.2, 1.6, ((0, 16),), jnp.float32)
    return dict(pixel_map=pixel_map, materials=materials, mode_panel=mode_panel)


exact_mode = lax.Precision.HIGHEST


def phase_table(first, second, period):
    turns = jnp.mod(first[:, None] * second[None, :], period)
    angle = turns.astype(jnp.float32) * (2.0 * math.pi / period)
    return jnp.cos(angle), jnp.sin(angle)


def complex_product(left_real, left_imag, right_real, right_imag):
    real = jnp.einsum("lmk,lkn->lmn", left_real, right_real, precision=exact_mode) - jnp.einsum("lmk,lkn->lmn", left_imag, right_imag, precision=exact_mode)
    imag = jnp.einsum("lmk,lkn->lmn", left_real, right_imag, precision=exact_mode) + jnp.einsum("lmk,lkn->lmn", left_imag, right_real, precision=exact_mode)
    return real, imag


def line_inverse(pixel_rows, materials):
    inverse_eps = jnp.zeros(pixel_rows.shape, jnp.float32)
    for material in range(NMAT):
        inverse_eps = inverse_eps + jnp.where(pixel_rows == material, 1.0 / materials[material], 0.0)
    orders = jnp.arange(2 * ORD - 1, dtype=jnp.int32) - (ORD - 1)
    pixels = jnp.arange(NPIX, dtype=jnp.int32)
    cosine, sine = phase_table(orders, pixels, NPIX)
    coef_real = jnp.einsum("lx,kx->lk", inverse_eps, cosine, precision=exact_mode) / NPIX
    coef_imag = -jnp.einsum("lx,kx->lk", inverse_eps, sine, precision=exact_mode) / NPIX
    offsets = (jnp.arange(ORD, dtype=jnp.int32)[:, None] - jnp.arange(ORD, dtype=jnp.int32)[None, :] + (ORD - 1)).astype(jnp.int32)
    toep_real = coef_real[:, offsets]
    toep_imag = coef_imag[:, offsets]
    factor = 2.0 / (1.0 / jnp.min(materials) + 1.0 / jnp.max(materials))
    identity = jnp.eye(ORD, dtype=jnp.float32)
    iterate_real = 2.0 * factor * identity - factor * factor * toep_real
    iterate_imag = -factor * factor * toep_imag
    for sweep in range(NS_ITERS - 1):
        inner_real, inner_imag = complex_product(toep_real, toep_imag, iterate_real, iterate_imag)
        outer_real, outer_imag = complex_product(iterate_real, iterate_imag, inner_real, inner_imag)
        iterate_real = 2.0 * iterate_real - outer_real
        iterate_imag = 2.0 * iterate_imag - outer_imag
    return iterate_real, iterate_imag


def reference(pixel_map, materials, mode_panel):
    inverse_real, inverse_imag = line_inverse(pixel_map, materials)
    lines = pixel_map.shape[0]
    half = (YORD - 1) // 2
    line_ids = jnp.arange(lines, dtype=jnp.int32)
    y_orders = jnp.arange(YORD, dtype=jnp.int32) - half
    cosine, sine = phase_table(line_ids, y_orders, lines)
    panel_real = mode_panel[:, 0]
    panel_imag = mode_panel[:, 1]
    spread_real = jnp.einsum("yp,cpn->cyn", cosine, panel_real, precision=exact_mode) - jnp.einsum("yp,cpn->cyn", sine, panel_imag, precision=exact_mode)
    spread_imag = jnp.einsum("yp,cpn->cyn", cosine, panel_imag, precision=exact_mode) + jnp.einsum("yp,cpn->cyn", sine, panel_real, precision=exact_mode)
    applied_real = jnp.einsum("ymn,cyn->cym", inverse_real, spread_real, precision=exact_mode) - jnp.einsum("ymn,cyn->cym", inverse_imag, spread_imag, precision=exact_mode)
    applied_imag = jnp.einsum("ymn,cyn->cym", inverse_real, spread_imag, precision=exact_mode) + jnp.einsum("ymn,cyn->cym", inverse_imag, spread_real, precision=exact_mode)
    out_real = (jnp.einsum("yp,cym->cpm", cosine, applied_real, precision=exact_mode) + jnp.einsum("yp,cym->cpm", sine, applied_imag, precision=exact_mode)) / lines
    out_imag = (jnp.einsum("yp,cym->cpm", cosine, applied_imag, precision=exact_mode) - jnp.einsum("yp,cym->cpm", sine, applied_real, precision=exact_mode)) / lines
    return jnp.stack([out_real, out_imag], axis=1)
```

```python
import functools
import math

import jax
import jax.numpy as jnp
import numpy as np
from jax import lax
from jax.experimental import pallas as pl
from jax.experimental.pallas import tpu as pltpu
from jax.sharding import PartitionSpec as P

NMAT = 4
NS_ITERS = 3
LANES = 128


def up(value, step):
    return -(-value // step) * step


def split(x):
    high = x.astype(jnp.bfloat16)
    low = (x - high.astype(jnp.float32)).astype(jnp.bfloat16)
    return high, low


def dot(a, b):
    return jnp.dot(a, b, preferred_element_type=jnp.float32)


def dot_split(a, b):
    return dot(a[0], b[0]) + dot(a[1], b[0]) + dot(a[0], b[1])


def split_table(table):
    table = np.asarray(table, np.float32)
    high = table.astype(jnp.bfloat16)
    low = (table - high.astype(np.float32)).astype(jnp.bfloat16)
    return np.stack([high, low])


def turn(product, period):
    return np.mod(product, period) * (2.0 * math.pi / period)


def pixel_tables(npix, order):
    width = up(order, LANES)
    k = np.arange(order)
    inner = np.zeros((LANES, 2 * width))
    angle = turn(np.arange(LANES)[:, None] * k[None, :], npix)
    inner[:, :order] = np.cos(angle) / npix
    inner[:, width : width + order] = np.sin(angle) / npix
    chunks = npix // LANES
    outer = np.zeros((chunks, 2 * width), np.float32)
    angle = turn(LANES * np.arange(chunks)[:, None] * k[None, :], npix)
    outer[:, :order] = np.cos(angle)
    outer[:, width : width + order] = np.sin(angle)
    return split_table(inner), outer


def symbol_table(order):
    width = up(order, LANES)
    k = np.arange(order)
    weight = np.where(k == 0, 1.0, 2.0)[:, None]
    table = np.zeros((2 * width, 2 * width))
    for half in range(2):
        angle = turn(k[:, None] * (2 * np.arange(order)[None, :] + half), 2 * order)
        columns = slice(half * width, half * width + order)
        table[:order, columns] = weight * np.cos(angle)
        table[width : width + order, columns] = weight * np.sin(angle)
    return split_table(table)


def order_tables(order, scale):
    width = up(order, LANES)
    centred = np.arange(order) - (order - 1) // 2
    whole = 2 * np.arange(order)
    angle = turn(centred[:, None] * whole[None, :], 2 * order)
    forward = np.zeros((width, 2 * width))
    forward[:order, :order] = np.cos(angle)
    forward[:order, width : width + order] = np.sin(angle)
    inverse = np.zeros((width, 2 * width))
    inverse[:order, :order] = np.cos(angle).T * (scale / order)
    inverse[:order, width : width + order] = np.sin(angle).T * (scale / order)
    gap = whole[:, None] - (whole + 1)[None, :]
    angle = turn(centred[:, None, None] * gap[None], 2 * order)
    step = np.zeros((width, width))
    step[:order, :order] = np.cos(angle).sum(0) / order
    return split_table(forward), split_table(inverse), split_table(step), split_table(step.T)


def line_tables(lines, yord, rows, kept):
    half = (yord - 1) // 2
    angle = turn(np.arange(lines)[:, None] * (np.arange(kept) - half)[None, :], lines)
    cosine, sine = np.zeros((lines, rows)), np.zeros((lines, rows))
    cosine[:, :kept], sine[:, :kept] = np.cos(angle), np.sin(angle)
    spread = np.block([[cosine, -sine], [sine, cosine]])
    return split_table(spread), split_table(spread.T)


def scale_of(materials):
    low = functools.reduce(jnp.minimum, materials)
    high = functools.reduce(jnp.maximum, materials)
    full = lambda value: jnp.full((1, LANES), value, jnp.float32)
    return 2.0 / (1.0 / full(low) + 1.0 / full(high))


def symbol_kernel(mats, pixels, inner, outer, table, out):
    materials = [mats[i] for i in range(NMAT)]
    inverse = [1.0 / jnp.full((1, LANES), m, jnp.float32) for m in materials]
    lines, npix = pixels.shape
    width = outer.shape[1] // 2
    chunks = npix // LANES
    parts = []
    for chunk in range(chunks):
        index = pixels[:, chunk * LANES : (chunk + 1) * LANES]
        value = jnp.zeros((lines, LANES), jnp.float32)
        for i in range(NMAT):
            value = value + jnp.where(index == i, inverse[i], 0.0)
        parts.append(value)
    inside = dot_split(split(jnp.concatenate(parts, 0)), (inner[0], inner[1]))
    real = jnp.zeros((lines, width), jnp.float32)
    imag = jnp.zeros((lines, width), jnp.float32)
    for chunk in range(chunks):
        rows = slice(chunk * lines, (chunk + 1) * lines)
        in_cos, in_sin = inside[rows, :width], inside[rows, width:]
        out_cos, out_sin = outer[chunk : chunk + 1, :width], outer[chunk : chunk + 1, width:]
        real = real + in_cos * out_cos - in_sin * out_sin
        imag = imag - in_cos * out_sin - in_sin * out_cos
    symbol = dot_split(split(jnp.concatenate([real, imag], 1)), (table[0], table[1]))
    out[...] = 0.5 - (0.5 * scale_of(materials)[0, 0]) * symbol


def panel_kernel(mats, symbol, panel, forward, inverse, step, back, to_lines, to_orders, out, folded, start, state):
    columns, _, yord, order = panel.shape
    rows = folded.shape[1] // 2
    lines = symbol.shape[0]
    kept = min(lines, yord)
    width = folded.shape[2]
    pair = lambda ref: (ref[0], ref[1])

    for c in range(columns):
        folded[c] = jnp.zeros((2 * rows, width), jnp.float32)
        for part in range(2):
            base = part * rows
            folded[c, base : base + kept, :order] = panel[c, part, :kept, :]
            for first in range(lines, yord, lines):
                count = min(lines, yord - first)
                folded[c, base : base + count, :order] += panel[c, part, first : first + count, :]
        both = dot_split(split(folded[c]), pair(forward))
        cosine, sine = both[:, :width], both[:, width:]
        real = cosine[:rows] + sine[rows:]
        imag = cosine[rows:] - sine[:rows]
        high, low = split(jnp.concatenate([real, imag], 0))
        value = dot(to_lines[0], high) + dot(to_lines[1], high) + dot(to_lines[0], low)
        start[c] = value
        state[c] = value

    def sweep(_, carry):
        whole = symbol[:, :width]
        half = symbol[:, width:]
        for c in range(columns):
            now = state[c]
            other = dot_split(split(now), pair(step))
            other = jnp.concatenate([other[:lines] * half, other[lines:] * half], 0)
            same = jnp.concatenate([now[:lines] * whole, now[lines:] * whole], 0)
            state[c] = start[c] + same + dot_split(split(other), pair(back))
        return carry

    lax.fori_loop(0, 2**NS_ITERS - 1, sweep, 0)

    factor = scale_of([mats[i] for i in range(NMAT)])[0, 0]
    for c in range(columns):
        high, low = split(state[c])
        value = dot(to_orders[0], high) + dot(to_orders[1], high) + dot(to_orders[0], low)
        both = dot_split(split(value * factor), pair(inverse))
        cosine, sine = both[:, :width], both[:, width:]
        real = cosine[:rows] - sine[rows:]
        imag = cosine[rows:] + sine[:rows]
        for part, value in enumerate((real, imag)):
            for first in range(0, yord, lines):
                count = min(lines, yord - first)
                out[c, part, first : first + count, :] = value[:count, :order]


SMEM = pl.BlockSpec(memory_space=pltpu.SMEM)
VMEM = pl.BlockSpec(memory_space=pltpu.VMEM)


def local(pixel_map, materials, mode_panel):
    devices = lax.axis_size("long")
    own, npix = pixel_map.shape
    lines = own * devices
    columns, _, yord, order = mode_panel.shape
    width = up(order, LANES)
    kept = min(lines, yord)
    rows = up(kept, 16)

    inner, outer = pixel_tables(npix, order)
    mine = pl.pallas_call(
        symbol_kernel,
        out_shape=jax.ShapeDtypeStruct((own, 2 * width), jnp.float32),
        in_specs=[SMEM] + [VMEM] * 4,
        out_specs=VMEM,
        name="symbol",
    )(materials, pixel_map, inner, outer, symbol_table(order))
    everyone = jnp.broadcast_to(mine[None], (devices,) + mine.shape)
    symbol = lax.all_to_all(everyone, "long", split_axis=0, concat_axis=0).reshape(lines, 2 * width)

    forward, inverse, step, back = order_tables(order, 1.0 / lines)
    to_lines, to_orders = line_tables(lines, yord, rows, kept)
    return pl.pallas_call(
        panel_kernel,
        out_shape=jax.ShapeDtypeStruct(mode_panel.shape, jnp.float32),
        in_specs=[SMEM] + [VMEM] * 8,
        out_specs=VMEM,
        scratch_shapes=[
            pltpu.VMEM((columns, 2 * rows, width), jnp.float32),
            pltpu.VMEM((columns, 2 * lines, width), jnp.float32),
            pltpu.VMEM((columns, 2 * lines, width), jnp.float32),
        ],
        compiler_params=pltpu.CompilerParams(vmem_limit_bytes=48 * 2**20),
        name="panel",
    )(materials, symbol, mode_panel, forward, inverse, step, back, to_lines, to_orders)


def solution(mesh):
    in_specs = (P(("grp", "long"), None), P("grp"), P(("grp", "long"), None, None, None))
    out_specs = P(("grp", "long"), None, None, None)
    return jax.shard_map(local, mesh=mesh, in_specs=in_specs, out_specs=out_specs, check_vma=False)
```

```python
import functools
import math

import jax
import jax.numpy as jnp
import numpy as np
from jax import lax
from jax.experimental import pallas as pl
from jax.experimental.pallas import tpu as pltpu
from jax.sharding import PartitionSpec as P

NMAT = 4
NS_ITERS = 3
LANES = 128
BLOCK = 128


def up(value, step):
    return -(-value // step) * step


def split(x):
    high = x.astype(jnp.bfloat16)
    low = (x - high.astype(jnp.float32)).astype(jnp.bfloat16)
    return high, low


def dot(a, b):
    return jnp.dot(a, b, preferred_element_type=jnp.float32)


def dot_split(a, b):
    return dot(a[0], b[0]) + dot(a[1], b[0]) + dot(a[0], b[1])


def split_table(table):
    table = np.asarray(table, np.float32)
    high = table.astype(jnp.bfloat16)
    low = (table - high.astype(np.float32)).astype(jnp.bfloat16)
    return np.stack([high, low])


def turn(product, period):
    return np.mod(product, period) * (2.0 * math.pi / period)


def pixel_tables(npix, order):
    width = up(order, LANES)
    k = np.arange(order)
    inner = np.zeros((LANES, 2 * width))
    angle = turn(np.arange(LANES)[:, None] * k[None, :], npix)
    inner[:, :order] = np.cos(angle) / npix
    inner[:, width : width + order] = np.sin(angle) / npix
    chunks = npix // LANES
    outer = np.zeros((chunks, 2 * width), np.float32)
    angle = turn(LANES * np.arange(chunks)[:, None] * k[None, :], npix)
    outer[:, :order] = np.cos(angle)
    outer[:, width : width + order] = np.sin(angle)
    return split_table(inner), outer


def symbol_table(order):
    width = up(order, LANES)
    k = np.arange(order)
    weight = np.where(k == 0, 1.0, 2.0)[:, None]
    table = np.zeros((2 * width, 2 * width))
    for half in range(2):
        angle = turn(k[:, None] * (2 * np.arange(order)[None, :] + half), 2 * order)
        columns = slice(half * width, half * width + order)
        table[:order, columns] = weight * np.cos(angle)
        table[width : width + order, columns] = weight * np.sin(angle)
    return split_table(table)


def order_tables(order, scale):
    width = up(order, LANES)
    centred = np.arange(order) - (order - 1) // 2
    whole = 2 * np.arange(order)
    angle = turn(centred[:, None] * whole[None, :], 2 * order)
    forward = np.zeros((width, 2 * width))
    forward[:order, :order] = np.cos(angle)
    forward[:order, width : width + order] = np.sin(angle)
    inverse = np.zeros((width, 2 * width))
    inverse[:order, :order] = np.cos(angle).T * (scale / order)
    inverse[:order, width : width + order] = np.sin(angle).T * (scale / order)
    gap = whole[:, None] - (whole + 1)[None, :]
    angle = turn(centred[:, None, None] * gap[None], 2 * order)
    step = np.zeros((width, width))
    step[:order, :order] = np.cos(angle).sum(0) / order
    return split_table(forward), split_table(inverse), split_table(step), split_table(step.T)


def line_tables(lines, yord, rows, kept):
    half = (yord - 1) // 2
    angle = turn(np.arange(lines)[:, None] * (np.arange(kept) - half)[None, :], lines)
    cosine, sine = np.zeros((lines, rows)), np.zeros((lines, rows))
    cosine[:, :kept], sine[:, :kept] = np.cos(angle), np.sin(angle)
    spread = np.block([[cosine, -sine], [sine, cosine]])
    return split_table(spread), split_table(spread.T)


def scale_of(materials):
    low = functools.reduce(jnp.minimum, materials)
    high = functools.reduce(jnp.maximum, materials)
    full = lambda value: jnp.full((1, LANES), value, jnp.float32)
    return 2.0 / (1.0 / full(low) + 1.0 / full(high))


def coefficient_kernel(mats, pixels, inner, outer, out):
    inverse = [1.0 / jnp.full((1, LANES), mats[i], jnp.float32) for i in range(NMAT)]
    lines, npix = pixels.shape
    width = outer.shape[1] // 2
    chunks = npix // LANES
    parts = []
    for chunk in range(chunks):
        index = pixels[:, chunk * LANES : (chunk + 1) * LANES]
        value = jnp.zeros((lines, LANES), jnp.float32)
        for i in range(NMAT):
            value = value + jnp.where(index == i, inverse[i], 0.0)
        parts.append(value)
    inside = dot_split(split(jnp.concatenate(parts, 0)), (inner[0], inner[1]))
    real = jnp.zeros((lines, width), jnp.float32)
    imag = jnp.zeros((lines, width), jnp.float32)
    for chunk in range(chunks):
        rows = slice(chunk * lines, (chunk + 1) * lines)
        in_cos, in_sin = inside[rows, :width], inside[rows, width:]
        out_cos, out_sin = outer[chunk : chunk + 1, :width], outer[chunk : chunk + 1, width:]
        real = real + in_cos * out_cos - in_sin * out_sin
        imag = imag - in_cos * out_sin - in_sin * out_cos
    out[:, :width] = real
    out[:, width:] = imag


def pair(ref):
    return ref[0], ref[1]


def spread_kernel(panel, forward, to_lines, out, folded):
    _, yord, _, order = panel.shape
    width = out.shape[1]
    rows = folded.shape[1] // 2
    double_lines = to_lines.shape[1]
    lines = double_lines // 2
    kept = min(lines, yord)
    for c in range(folded.shape[0]):
        folded[c] = jnp.zeros((2 * rows, width), jnp.float32)
        for part in range(2):
            base = part * rows
            folded[c, base : base + kept, :order] = panel[c, :kept, part, :]
            for first in range(lines, yord, lines):
                count = min(lines, yord - first)
                folded[c, base : base + count, :order] += panel[c, first : first + count, part, :]
        both = dot_split(split(folded[c]), pair(forward))
        cosine, sine = both[:, :width], both[:, width:]
        real = cosine[:rows] + sine[rows:]
        imag = cosine[rows:] - sine[:rows]
        high, low = split(jnp.concatenate([real, imag], 0))
        value = dot(to_lines[0], high) + dot(to_lines[1], high) + dot(to_lines[0], low)
        out[c * double_lines : (c + 1) * double_lines, :] = value


def sweeps(count, half, start_of, symbol, steps, state, now, other, sums):
    lines, width = symbol.shape[0], state.shape[1]
    blocks = half // BLOCK
    per_section = blocks // 2

    def rows(unit, block):
        return slice(unit * half + block * BLOCK, unit * half + (block + 1) * BLOCK)

    def symbol_rows(unit, block, part):
        first = (unit * half + block * BLOCK) % lines
        return symbol[first : first + BLOCK, part * width : (part + 1) * width]

    def issue(stage, section):
        high, low = now if stage == 0 else other
        own = range(section * per_section, (section + 1) * per_section)
        for unit in range(2):
            for part in range(2):
                pltpu.matmul_push_rhs(steps[2 * stage + part], part, unit)
        for block in own:
            for unit in range(2):
                load = 0 if block == own[0] else None
                pltpu.matmul_acc_lhs(sums[unit * blocks + block], high[rows(unit, block)], load_staged_rhs=load)
                pltpu.matmul_acc_lhs(sums[unit * blocks + block], low[rows(unit, block)])
        for block in own:
            for unit in range(2):
                load = 1 if block == own[0] else None
                pltpu.matmul_acc_lhs(sums[unit * blocks + block], high[rows(unit, block)], load_staged_rhs=load)

    def finish(stage, section):
        for block in range(section * per_section, (section + 1) * per_section):
            for unit in range(2):
                place = rows(unit, block)
                value = pltpu.matmul_pop(sums[unit * blocks + block])
                if stage == 0:
                    high, low = split(value * symbol_rows(unit, block, 1))
                    other[0][place], other[1][place] = high, low
                else:
                    value = start_of(unit, block) + state[place] * symbol_rows(unit, block, 0) + value
                    state[place] = value
                    now[0][place], now[1][place] = split(value)

    def sweep(last):
        order = ((0, 0), (0, 1), (1, 0), (1, 1))
        for index, unit in enumerate(order):
            if index + 1 < len(order):
                issue(*order[index + 1])
            elif not last:
                issue(*order[0])
            finish(*unit)

    issue(0, 0)
    lax.fori_loop(0, count - 1, lambda _, carry: (sweep(False), carry)[1], 0)
    sweep(True)


def unit_product(lhs, rhs, unit, sums):
    depth = lhs[0].shape[1]
    tile = sums.shape[1]
    for first in range(0, depth, tile):
        inner = slice(first, first + tile)
        for part in range(2):
            pltpu.matmul_push_rhs(rhs[part][inner], part, unit)
        pltpu.matmul_acc_lhs(sums, lhs[0][:, inner], load_staged_rhs=0)
        pltpu.matmul_acc_lhs(sums, lhs[1][:, inner])
        pltpu.matmul_acc_lhs(sums, lhs[0][:, inner], load_staged_rhs=1)
    return pltpu.matmul_pop(sums)


def apply_kernel(groups, owners, mats, me, *refs):
    starts, refs = refs[:groups], refs[groups:]
    pieces, refs = refs[: len(owners)], refs[len(owners) :]
    table, steps, inverse, to_orders, out, coefficients, symbol, state, result, ready, *splits = refs
    now, other = splits[:2], splits[2:]
    columns, yord, _, order = out.shape
    lines = coefficients.shape[0]
    width = state.shape[1]
    rows = to_orders.shape[1] // 2
    half = state.shape[0] // 2
    factor = scale_of([mats[i] for i in range(NMAT)])[0, 0]

    for piece, ids in zip(pieces, owners):
        own = piece.shape[0] // len(ids)
        for index, distance in enumerate(ids):
            place = pl.multiple_of((me[0] ^ distance) * own, own)
            coefficients[pl.ds(place, own), :] = piece[index * own : (index + 1) * own]
    values = split(coefficients[...])

    def all_symbols(*sums):
        for unit in range(2):
            columns_of = slice(unit * width, (unit + 1) * width)
            value = unit_product(values, (table.at[0, :, columns_of], table.at[1, :, columns_of]), unit, sums[unit])
            symbol[:, columns_of] = 0.5 - (0.5 * factor) * value

    pl.run_scoped(all_symbols, *[pltpu.ACC(unit)((lines, width), jnp.float32) for unit in range(2)])

    share = state.shape[0] // groups
    for group in range(groups):
        place = slice(group * share, (group + 1) * share)
        value = starts[group][...]
        state[place] = value
        now[0][place], now[1][place] = split(value)

    def start_of(unit, block):
        first = unit * half + block * BLOCK
        return starts[first // share][first % share : first % share + BLOCK]

    def run(*sums):
        sweeps(2**NS_ITERS - 1, half, start_of, symbol, steps, state, now, other, sums)

    pl.run_scoped(run, *[pltpu.ACC(unit)((BLOCK, width), jnp.float32) for unit in range(2) for _ in range(half // BLOCK)])

    def finish(*sums):
        for c in range(columns):
            place = slice(c * 2 * lines, (c + 1) * 2 * lines)
            data = now[0].at[place], now[1].at[place]
            value = unit_product((to_orders[0], to_orders[1]), data, c % 2, sums[c % 2])
            value = split(value * factor)
            cosine, sine = (
                unit_product(
                    value,
                    tuple(inverse.at[part, :, unit * width : (unit + 1) * width] for part in range(2)),
                    unit,
                    sums[2 + 2 * (c % buffers) + unit],
                )
                for unit in range(2)
            )
            real = cosine[:rows] - sine[rows:]
            imag = cosine[rows:] + sine[:rows]
            for part, value in enumerate((real, imag)):
                for first in range(0, yord, lines):
                    count = min(lines, yord - first)
                    result[c, first : first + count, part, :] = value[:count, :order]
            pltpu.make_async_copy(result.at[c], out.at[c], ready.at[c]).start()
        for c in range(columns):
            pltpu.make_async_copy(result.at[c], out.at[c], ready.at[c]).wait()

    buffers = min(2, columns)
    pl.run_scoped(finish, *[pltpu.ACC(i % 2)((2 * rows, width), jnp.float32) for i in range(2 + 2 * buffers)])


SMEM = pl.BlockSpec(memory_space=pltpu.SMEM)
VMEM = pl.BlockSpec(memory_space=pltpu.VMEM)


def local(pixel_map, materials, mode_panel):
    devices = lax.axis_size("long")
    own, npix = pixel_map.shape
    lines = own * devices
    columns, _, yord, order = mode_panel.shape
    width = up(order, LANES)
    kept = min(lines, yord)
    rows = up(kept, 16)
    groups = 2 if columns % 2 == 0 else 1
    share = columns // groups
    total = columns * 2 * lines
    limit = pltpu.CompilerParams(vmem_limit_bytes=24 * 2**20)

    inner, outer = pixel_tables(npix, order)
    mine = pl.pallas_call(
        coefficient_kernel,
        out_shape=jax.ShapeDtypeStruct((own, 2 * width), jnp.float32),
        in_specs=[SMEM] + [VMEM] * 3,
        out_specs=VMEM,
        cost_estimate=pl.CostEstimate(flops=3 * 10**9, bytes_accessed=2**22, transcendentals=0),
        name="coefficient",
    )(materials, pixel_map, inner, outer)

    forward, inverse, step, back = order_tables(order, 1.0 / lines)
    to_lines, to_orders = line_tables(lines, yord, rows, kept)

    pieces, owners, starts = [mine], [(0,)], []
    by_order = jnp.swapaxes(mode_panel, 1, 2)
    distance = devices // 2
    while distance:
        held = jnp.concatenate(pieces, 0) if len(pieces) > 1 else mine
        other = lax.ppermute(held, "long", [(i, i ^ distance) for i in range(devices)])
        if len(starts) < groups:
            group = len(starts)
            start = pl.pallas_call(
                spread_kernel,
                grid=(1,),
                out_shape=jax.ShapeDtypeStruct((share * 2 * lines, width), jnp.float32),
                in_specs=[pl.BlockSpec((share, yord, 2, order), lambda _, group=group: (group, 0, 0, 0)), VMEM, VMEM],
                out_specs=VMEM,
                scratch_shapes=[pltpu.VMEM((share, 2 * rows, width), jnp.float32)],
                compiler_params=limit,
                cost_estimate=pl.CostEstimate(flops=10**9, bytes_accessed=2**21, transcendentals=0),
                name="spread",
            )(by_order, forward, to_lines)
            start, other = lax.optimization_barrier((start, other))
            starts.append(start)
        owners.append(tuple(d ^ distance for ids in owners for d in ids))
        pieces.append(other)
        distance //= 2

    half = [pltpu.VMEM((total, width), jnp.bfloat16)]
    result = pl.pallas_call(
        functools.partial(apply_kernel, groups, owners),
        out_shape=jax.ShapeDtypeStruct(by_order.shape, jnp.float32),
        in_specs=[SMEM, SMEM] + [VMEM] * (4 + groups + len(pieces)),
        out_specs=pl.BlockSpec(memory_space=pl.ANY),
        scratch_shapes=[
            pltpu.VMEM((lines, 2 * width), jnp.float32),
            pltpu.VMEM((lines, 2 * width), jnp.float32),
            pltpu.VMEM((total, width), jnp.float32),
            pltpu.VMEM(by_order.shape, jnp.float32),
            pltpu.SemaphoreType.DMA((columns,)),
        ]
        + half * 4,
        compiler_params=limit,
        name="apply",
    )(
        materials,
        jnp.full((1,), lax.axis_index("long"), jnp.int32),
        *starts,
        *pieces,
        symbol_table(order),
        np.concatenate([step, back]),
        inverse,
        to_orders,
    )
    return jnp.swapaxes(result, 1, 2)


def solution(mesh):
    in_specs = (P(("grp", "long"), None), P("grp"), P(("grp", "long"), None, None, None))
    out_specs = P(("grp", "long"), None, None, None)
    return jax.shard_map(local, mesh=mesh, in_specs=in_specs, out_specs=out_specs, check_vma=False)
```

```python
import functools
import math

import jax
import jax.numpy as jnp
import numpy as np
from jax import lax
from jax.experimental import pallas as pl
from jax.experimental.pallas import tpu as pltpu
from jax.sharding import PartitionSpec as P

NMAT = 4
NS_ITERS = 3
LANES = 128
BLOCK = 128


def up(value, step):
    return -(-value // step) * step


def split(x):
    high = x.astype(jnp.bfloat16)
    low = (x - high.astype(jnp.float32)).astype(jnp.bfloat16)
    return high, low


def dot(a, b):
    return jnp.dot(a, b, preferred_element_type=jnp.float32)


def dot_split(a, b):
    return dot(a[0], b[0]) + dot(a[1], b[0]) + dot(a[0], b[1])


def split_table(table):
    table = np.asarray(table, np.float32)
    high = table.astype(jnp.bfloat16)
    low = (table - high.astype(np.float32)).astype(jnp.bfloat16)
    return np.stack([high, low])


def turn(product, period):
    return np.mod(product, period) * (2.0 * math.pi / period)


def pixel_tables(npix, order):
    width = up(order, LANES)
    k = np.arange(order)
    inner = np.zeros((LANES, 2 * width))
    angle = turn(np.arange(LANES)[:, None] * k[None, :], npix)
    inner[:, :order] = np.cos(angle) / npix
    inner[:, width : width + order] = np.sin(angle) / npix
    chunks = npix // LANES
    outer = np.zeros((chunks, 2 * width), np.float32)
    angle = turn(LANES * np.arange(chunks)[:, None] * k[None, :], npix)
    outer[:, :order] = np.cos(angle)
    outer[:, width : width + order] = np.sin(angle)
    return split_table(inner), outer


def symbol_table(order):
    width = up(order, LANES)
    k = np.arange(order)
    weight = np.where(k == 0, 1.0, 2.0)[:, None]
    table = np.zeros((2 * width, 2 * width))
    for half in range(2):
        angle = turn(k[:, None] * (2 * np.arange(order)[None, :] + half), 2 * order)
        columns = slice(half * width, half * width + order)
        table[:order, columns] = weight * np.cos(angle)
        table[width : width + order, columns] = weight * np.sin(angle)
    return split_table(table)


def order_tables(order, scale):
    width = up(order, LANES)
    centred = np.arange(order) - (order - 1) // 2
    whole = 2 * np.arange(order)
    angle = turn(centred[:, None] * whole[None, :], 2 * order)
    forward = np.zeros((width, 2 * width))
    forward[:order, :order] = np.cos(angle)
    forward[:order, width : width + order] = np.sin(angle)
    inverse = np.zeros((width, 2 * width))
    inverse[:order, :order] = np.cos(angle).T * (scale / order)
    inverse[:order, width : width + order] = np.sin(angle).T * (scale / order)
    gap = whole[:, None] - (whole + 1)[None, :]
    angle = turn(centred[:, None, None] * gap[None], 2 * order)
    step = np.zeros((width, width))
    step[:order, :order] = np.cos(angle).sum(0) / order
    return split_table(forward), split_table(inverse), split_table(step), split_table(step.T)


def line_tables(lines, yord, rows, kept):
    half = (yord - 1) // 2
    angle = turn(np.arange(lines)[:, None] * (np.arange(kept) - half)[None, :], lines)
    cosine, sine = np.zeros((lines, rows)), np.zeros((lines, rows))
    cosine[:, :kept], sine[:, :kept] = np.cos(angle), np.sin(angle)
    spread = np.block([[cosine, -sine], [sine, cosine]])
    return split_table(spread), split_table(spread.T)


def scale_of(materials):
    low = functools.reduce(jnp.minimum, materials)
    high = functools.reduce(jnp.maximum, materials)
    full = lambda value: jnp.full((1, LANES), value, jnp.float32)
    return 2.0 / (1.0 / full(low) + 1.0 / full(high))


def coefficient_kernel(mats, pixels, inner, outer, out):
    inverse = [1.0 / jnp.full((1, LANES), mats[i], jnp.float32) for i in range(NMAT)]
    lines, npix = pixels.shape
    width = outer.shape[1] // 2
    chunks = npix // LANES
    parts = []
    for chunk in range(chunks):
        index = pixels[:, chunk * LANES : (chunk + 1) * LANES]
        value = jnp.zeros((lines, LANES), jnp.float32)
        for i in range(NMAT):
            value = value + jnp.where(index == i, inverse[i], 0.0)
        parts.append(value)
    inside = dot_split(split(jnp.concatenate(parts, 0)), (inner[0], inner[1]))
    real = jnp.zeros((lines, width), jnp.float32)
    imag = jnp.zeros((lines, width), jnp.float32)
    for chunk in range(chunks):
        rows = slice(chunk * lines, (chunk + 1) * lines)
        in_cos, in_sin = inside[rows, :width], inside[rows, width:]
        out_cos, out_sin = outer[chunk : chunk + 1, :width], outer[chunk : chunk + 1, width:]
        real = real + in_cos * out_cos - in_sin * out_sin
        imag = imag - in_cos * out_sin - in_sin * out_cos
    out[:, :width] = real
    out[:, width:] = imag


def pair(ref):
    return ref[0], ref[1]


def spread_kernel(panel, forward, to_lines, out, folded):
    _, yord, _, order = panel.shape
    width = out.shape[1]
    rows = folded.shape[1] // 2
    double_lines = to_lines.shape[1]
    lines = double_lines // 2
    kept = min(lines, yord)
    for c in range(folded.shape[0]):
        folded[c] = jnp.zeros((2 * rows, width), jnp.float32)
        for part in range(2):
            base = part * rows
            folded[c, base : base + kept, :order] = panel[c, :kept, part, :]
            for first in range(lines, yord, lines):
                count = min(lines, yord - first)
                folded[c, base : base + count, :order] += panel[c, first : first + count, part, :]
        both = dot_split(split(folded[c]), pair(forward))
        cosine, sine = both[:, :width], both[:, width:]
        real = cosine[:rows] + sine[rows:]
        imag = cosine[rows:] - sine[:rows]
        high, low = split(jnp.concatenate([real, imag], 0))
        value = dot(to_lines[0], high) + dot(to_lines[1], high) + dot(to_lines[0], low)
        out[c * double_lines : (c + 1) * double_lines, :] = value


def sweeps(count, half, start_of, symbol, steps, state, now, other, sums):
    lines, width = symbol.shape[0], state.shape[1]
    blocks = half // BLOCK
    per_section = blocks // 2

    def rows(unit, block):
        return slice(unit * half + block * BLOCK, unit * half + (block + 1) * BLOCK)

    def symbol_rows(unit, block, part):
        first = (unit * half + block * BLOCK) % lines
        return symbol[first : first + BLOCK, part * width : (part + 1) * width]

    def issue(stage, section):
        high, low = now if stage == 0 else other
        own = range(section * per_section, (section + 1) * per_section)
        for unit in range(2):
            for part in range(2):
                pltpu.matmul_push_rhs(steps[2 * stage + part], part, unit)
        for block in own:
            for unit in range(2):
                load = 0 if block == own[0] else None
                pltpu.matmul_acc_lhs(sums[unit * blocks + block], high[rows(unit, block)], load_staged_rhs=load)
                pltpu.matmul_acc_lhs(sums[unit * blocks + block], low[rows(unit, block)])
        for block in own:
            for unit in range(2):
                load = 1 if block == own[0] else None
                pltpu.matmul_acc_lhs(sums[unit * blocks + block], high[rows(unit, block)], load_staged_rhs=load)

    def finish(stage, section):
        for block in range(section * per_section, (section + 1) * per_section):
            for unit in range(2):
                place = rows(unit, block)
                value = pltpu.matmul_pop(sums[unit * blocks + block])
                if stage == 0:
                    high, low = split(value * symbol_rows(unit, block, 1))
                    other[0][place], other[1][place] = high, low
                else:
                    value = start_of(unit, block) + state[place] * symbol_rows(unit, block, 0) + value
                    state[place] = value
                    now[0][place], now[1][place] = split(value)

    def sweep(last):
        order = ((0, 0), (0, 1), (1, 0), (1, 1))
        for index, unit in enumerate(order):
            if index + 1 < len(order):
                issue(*order[index + 1])
            elif not last:
                issue(*order[0])
            finish(*unit)

    issue(0, 0)
    lax.fori_loop(0, count - 1, lambda _, carry: (sweep(False), carry)[1], 0)
    sweep(True)


def unit_product(lhs, rhs, unit, sums):
    depth = lhs[0].shape[1]
    tile = sums.shape[1]
    for first in range(0, depth, tile):
        inner = slice(first, first + tile)
        for part in range(2):
            pltpu.matmul_push_rhs(rhs[part][inner], part, unit)
        pltpu.matmul_acc_lhs(sums, lhs[0][:, inner], load_staged_rhs=0)
        pltpu.matmul_acc_lhs(sums, lhs[1][:, inner])
        pltpu.matmul_acc_lhs(sums, lhs[0][:, inner], load_staged_rhs=1)
    return pltpu.matmul_pop(sums)


def apply_kernel(groups, owners, mats, me, *refs):
    starts, refs = refs[:groups], refs[groups:]
    pieces, refs = refs[: len(owners)], refs[len(owners) :]
    table, steps, inverse, to_orders, out, coefficients, symbol, state, result, ready, *splits = refs
    now, other = splits[:2], splits[2:]
    columns, yord, _, order = out.shape
    lines = coefficients.shape[0]
    width = state.shape[1]
    rows = to_orders.shape[1] // 2
    half = state.shape[0] // 2
    factor = scale_of([mats[i] for i in range(NMAT)])[0, 0]

    for piece, ids in zip(pieces, owners):
        own = piece.shape[0] // len(ids)
        for index, distance in enumerate(ids):
            place = pl.multiple_of((me[0] ^ distance) * own, own)
            coefficients[pl.ds(place, own), :] = piece[index * own : (index + 1) * own]
    values = split(coefficients[...])

    def all_symbols(*sums):
        for unit in range(2):
            columns_of = slice(unit * width, (unit + 1) * width)
            value = unit_product(values, (table.at[0, :, columns_of], table.at[1, :, columns_of]), unit, sums[unit])
            symbol[:, columns_of] = 0.5 - (0.5 * factor) * value

    pl.run_scoped(all_symbols, *[pltpu.ACC(unit)((lines, width), jnp.float32) for unit in range(2)])

    share = state.shape[0] // groups
    for group in range(groups):
        place = slice(group * share, (group + 1) * share)
        value = starts[group][...]
        state[place] = value
        now[0][place], now[1][place] = split(value)

    def start_of(unit, block):
        first = unit * half + block * BLOCK
        return starts[first // share][first % share : first % share + BLOCK]

    def run(*sums):
        sweeps(2**NS_ITERS - 1, half, start_of, symbol, steps, state, now, other, sums)

    pl.run_scoped(run, *[pltpu.ACC(unit)((BLOCK, width), jnp.float32) for unit in range(2) for _ in range(half // BLOCK)])

    def finish(*sums):
        for c in range(columns):
            place = slice(c * 2 * lines, (c + 1) * 2 * lines)
            data = now[0].at[place], now[1].at[place]
            value = unit_product((to_orders[0], to_orders[1]), data, c % 2, sums[c % 2])
            value = split(value * factor)
            cosine, sine = (
                unit_product(
                    value,
                    tuple(inverse.at[part, :, unit * width : (unit + 1) * width] for part in range(2)),
                    unit,
                    sums[2 + 2 * (c % buffers) + unit],
                )
                for unit in range(2)
            )
            real = cosine[:rows] - sine[rows:]
            imag = cosine[rows:] + sine[:rows]
            for part, value in enumerate((real, imag)):
                for first in range(0, yord, lines):
                    count = min(lines, yord - first)
                    result[c, first : first + count, part, :] = value[:count, :order]
            pltpu.make_async_copy(result.at[c], out.at[c], ready.at[c]).start()
        for c in range(columns):
            pltpu.make_async_copy(result.at[c], out.at[c], ready.at[c]).wait()

    buffers = min(2, columns)
    pl.run_scoped(finish, *[pltpu.ACC(i % 2)((2 * rows, width), jnp.float32) for i in range(2 + 2 * buffers)])


SMEM = pl.BlockSpec(memory_space=pltpu.SMEM)
VMEM = pl.BlockSpec(memory_space=pltpu.VMEM)


def join_kernel(*refs):
    first = 0
    for piece in refs[:-1]:
        refs[-1][first : first + piece.shape[0], :] = piece[...]
        first += piece.shape[0]


def join(pieces):
    rows = sum(piece.shape[0] for piece in pieces)
    return pl.pallas_call(
        join_kernel,
        out_shape=jax.ShapeDtypeStruct((rows, pieces[0].shape[1]), jnp.float32),
        in_specs=[VMEM] * len(pieces),
        out_specs=VMEM,
        compiler_params=pltpu.CompilerParams(vmem_limit_bytes=4 * 2**20),
        cost_estimate=pl.CostEstimate(flops=0, bytes_accessed=8 * rows * pieces[0].shape[1], transcendentals=0),
        name="join",
    )(*pieces)


def local(pixel_map, materials, mode_panel):
    devices = lax.axis_size("long")
    own, npix = pixel_map.shape
    lines = own * devices
    columns, _, yord, order = mode_panel.shape
    width = up(order, LANES)
    kept = min(lines, yord)
    rows = up(kept, 16)
    groups = 2 if columns % 2 == 0 else 1
    share = columns // groups
    total = columns * 2 * lines
    limit = pltpu.CompilerParams(vmem_limit_bytes=4 * 2**20)

    inner, outer = pixel_tables(npix, order)
    mine = pl.pallas_call(
        coefficient_kernel,
        out_shape=jax.ShapeDtypeStruct((own, 2 * width), jnp.float32),
        in_specs=[SMEM] + [VMEM] * 3,
        out_specs=VMEM,
        compiler_params=pltpu.CompilerParams(vmem_limit_bytes=56 * 2**20),
        cost_estimate=pl.CostEstimate(flops=3 * 10**9, bytes_accessed=2**22, transcendentals=0),
        name="coefficient",
    )(materials, pixel_map, inner, outer)

    forward, inverse, step, back = order_tables(order, 1.0 / lines)
    to_lines, to_orders = line_tables(lines, yord, rows, kept)

    def exchange(block, distance):
        return lax.ppermute(block, "long", [(i, i ^ distance) for i in range(devices)])

    by_order = jnp.swapaxes(mode_panel, 1, 2)
    pieces, owners, starts = [mine], [(0,)], []
    distance = devices // 2
    while distance > 1:
        held = join(pieces) if len(pieces) > 1 else mine
        ids = tuple(d for piece in owners for d in piece)
        other = exchange(held, distance)
        if len(starts) < groups:
            group = len(starts)
            start = pl.pallas_call(
                spread_kernel,
                grid=(1,),
                out_shape=jax.ShapeDtypeStruct((share * 2 * lines, width), jnp.float32),
                in_specs=[pl.BlockSpec((share, yord, 2, order), lambda _, group=group: (group, 0, 0, 0)), VMEM, VMEM],
                out_specs=VMEM,
                scratch_shapes=[pltpu.VMEM((share, 2 * rows, width), jnp.float32)],
                compiler_params=limit,
                cost_estimate=pl.CostEstimate(flops=10**9, bytes_accessed=2**21, transcendentals=0),
                name="spread",
            )(by_order, forward, to_lines)
            start, other = lax.optimization_barrier((start, other))
            starts.append(start)
        if distance == 2:
            beside = exchange(held, 1)
            pieces = [held, beside, other, exchange(other, 1)]
            owners = [ids, tuple(d ^ 1 for d in ids), tuple(d ^ 2 for d in ids), tuple(d ^ 3 for d in ids)]
        else:
            pieces.append(other)
            owners.append(tuple(d ^ distance for d in ids))
        distance //= 2

    half = [pltpu.VMEM((total, width), jnp.bfloat16)]
    result = pl.pallas_call(
        functools.partial(apply_kernel, groups, owners),
        out_shape=jax.ShapeDtypeStruct(by_order.shape, jnp.float32),
        in_specs=[SMEM, SMEM] + [VMEM] * (4 + groups + len(pieces)),
        out_specs=pl.BlockSpec(memory_space=pl.ANY),
        scratch_shapes=[
            pltpu.VMEM((lines, 2 * width), jnp.float32),
            pltpu.VMEM((lines, 2 * width), jnp.float32),
            pltpu.VMEM((total, width), jnp.float32),
            pltpu.VMEM(by_order.shape, jnp.float32),
            pltpu.SemaphoreType.DMA((columns,)),
        ]
        + half * 4,
        compiler_params=pltpu.CompilerParams(vmem_limit_bytes=10 * 2**20),
        cost_estimate=pl.CostEstimate(flops=1000000000, bytes_accessed=4194304, transcendentals=0),
        name="apply",
    )(
        materials,
        jnp.full((1,), lax.axis_index("long"), jnp.int32),
        *starts,
        *pieces,
        symbol_table(order),
        np.concatenate([step, back]),
        inverse,
        to_orders,
    )
    return jnp.swapaxes(result, 1, 2)


def solution(mesh):
    in_specs = (P(("grp", "long"), None), P("grp"), P(("grp", "long"), None, None, None))
    out_specs = P(("grp", "long"), None, None, None)
    return jax.shard_map(local, mesh=mesh, in_specs=in_specs, out_specs=out_specs, check_vma=False)
```

```python
import functools
import math

import jax
import jax.numpy as jnp
import numpy as np
from jax import lax
from jax.experimental import pallas as pl
from jax.experimental.pallas import tpu as pltpu
from jax.sharding import PartitionSpec as P

NMAT = 4
NS_ITERS = 3
LANES = 128
BLOCK = 128
SUM_ROWS = 1024


def up(value, step):
    return -(-value // step) * step


def split(x):
    high = x.astype(jnp.bfloat16)
    low = (x - high.astype(jnp.float32)).astype(jnp.bfloat16)
    return high, low


def dot(a, b):
    return jnp.dot(a, b, preferred_element_type=jnp.float32)


def dot_split(a, b):
    return dot(a[0], b[0]) + dot(a[1], b[0]) + dot(a[0], b[1])


def split_table(table):
    table = np.asarray(table, np.float32)
    high = table.astype(jnp.bfloat16)
    low = (table - high.astype(np.float32)).astype(jnp.bfloat16)
    return np.stack([high, low])


def turn(product, period):
    return np.mod(product, period) * (2.0 * math.pi / period)


def pixel_tables(npix, order):
    width = up(order, LANES)
    k = np.arange(order)
    inner = np.zeros((LANES, 2 * width))
    angle = turn(np.arange(LANES)[:, None] * k[None, :], npix)
    inner[:, :order] = np.cos(angle) / npix
    inner[:, width : width + order] = np.sin(angle) / npix
    chunks = npix // LANES
    outer = np.zeros((chunks, 2 * width), np.float32)
    angle = turn(LANES * np.arange(chunks)[:, None] * k[None, :], npix)
    outer[:, :order] = np.cos(angle)
    outer[:, width : width + order] = np.sin(angle)
    return split_table(inner), outer


def symbol_table(order):
    width = up(order, LANES)
    k = np.arange(order)
    weight = np.where(k == 0, 1.0, 2.0)[:, None]
    table = np.zeros((2 * width, 2 * width))
    for half in range(2):
        angle = turn(k[:, None] * (2 * np.arange(order)[None, :] + half), 2 * order)
        columns = slice(half * width, half * width + order)
        table[:order, columns] = weight * np.cos(angle)
        table[width : width + order, columns] = weight * np.sin(angle)
    return split_table(table)


def order_tables(order, scale):
    width = up(order, LANES)
    centred = np.arange(order) - (order - 1) // 2
    whole = 2 * np.arange(order)
    angle = turn(centred[:, None] * whole[None, :], 2 * order)
    forward = np.zeros((width, 2 * width))
    forward[:order, :order] = np.cos(angle)
    forward[:order, width : width + order] = np.sin(angle)
    inverse = np.zeros((width, 2 * width))
    inverse[:order, :order] = np.cos(angle).T * (scale / order)
    inverse[:order, width : width + order] = np.sin(angle).T * (scale / order)
    gap = whole[:, None] - (whole + 1)[None, :]
    angle = turn(centred[:, None, None] * gap[None], 2 * order)
    step = np.zeros((width, width))
    step[:order, :order] = np.cos(angle).sum(0) / order
    return split_table(forward), split_table(inverse), split_table(step), split_table(step.T)


def line_tables(lines, yord, rows, kept):
    half = (yord - 1) // 2
    angle = turn(np.arange(lines)[:, None] * (np.arange(kept) - half)[None, :], lines)
    cosine, sine = np.zeros((lines, rows)), np.zeros((lines, rows))
    cosine[:, :kept], sine[:, :kept] = np.cos(angle), np.sin(angle)
    spread = np.block([[cosine, -sine], [sine, cosine]])
    return split_table(spread), split_table(spread.T)


def scale_of(materials):
    low = functools.reduce(jnp.minimum, materials)
    high = functools.reduce(jnp.maximum, materials)
    full = lambda value: jnp.full((1, LANES), value, jnp.float32)
    return 2.0 / (1.0 / full(low) + 1.0 / full(high))


def coefficient_kernel(mats, pixels, inner, outer, out):
    inverse = [1.0 / jnp.full((1, LANES), mats[i], jnp.float32) for i in range(NMAT)]
    lines, npix = pixels.shape
    width = outer.shape[1] // 2
    chunks = npix // LANES
    parts = []
    for chunk in range(chunks):
        index = pixels[:, chunk * LANES : (chunk + 1) * LANES]
        value = jnp.zeros((lines, LANES), jnp.float32)
        for i in range(NMAT):
            value = value + jnp.where(index == i, inverse[i], 0.0)
        parts.append(value)
    inside = dot_split(split(jnp.concatenate(parts, 0)), (inner[0], inner[1]))
    real = jnp.zeros((lines, width), jnp.float32)
    imag = jnp.zeros((lines, width), jnp.float32)
    for chunk in range(chunks):
        rows = slice(chunk * lines, (chunk + 1) * lines)
        in_cos, in_sin = inside[rows, :width], inside[rows, width:]
        out_cos, out_sin = outer[chunk : chunk + 1, :width], outer[chunk : chunk + 1, width:]
        real = real + in_cos * out_cos - in_sin * out_sin
        imag = imag - in_cos * out_sin - in_sin * out_cos
    out[:, :width] = real
    out[:, width:] = imag


def pair(ref):
    return ref[0], ref[1]


def spread_kernel(panel, forward, to_lines, out, folded):
    _, yord, _, order = panel.shape
    width = out.shape[1]
    rows = folded.shape[1] // 2
    double_lines = to_lines.shape[1]
    lines = double_lines // 2
    kept = min(lines, yord)
    for c in range(folded.shape[0]):
        folded[c] = jnp.zeros((2 * rows, width), jnp.float32)
        for part in range(2):
            base = part * rows
            folded[c, base : base + kept, :order] = panel[c, :kept, part, :]
            for first in range(lines, yord, lines):
                count = min(lines, yord - first)
                folded[c, base : base + count, :order] += panel[c, first : first + count, part, :]
        both = dot_split(split(folded[c]), pair(forward))
        cosine, sine = both[:, :width], both[:, width:]
        real = cosine[:rows] + sine[rows:]
        imag = cosine[rows:] - sine[:rows]
        high, low = split(jnp.concatenate([real, imag], 0))
        value = dot(to_lines[0], high) + dot(to_lines[1], high) + dot(to_lines[0], low)
        out[c * double_lines : (c + 1) * double_lines, :] = value


def sweeps(count, half, start_of, first_of, symbol, steps, state, now, other, sums, done):
    lines, width = symbol.shape[0], state.shape[1]
    blocks = half // BLOCK
    per_section = blocks // 2

    def rows(unit, block):
        return slice(unit * half + block * BLOCK, unit * half + (block + 1) * BLOCK)

    def symbol_rows(unit, block, part):
        first = (unit * half + block * BLOCK) % lines
        return symbol[first : first + BLOCK, part * width : (part + 1) * width]

    def issue(stage, section):
        high, low = now if stage == 0 else other
        own = range(section * per_section, (section + 1) * per_section)
        for unit in range(2):
            for part in range(2):
                pltpu.matmul_push_rhs(steps[2 * stage + part], part, unit)
        for block in own:
            for unit in range(2):
                load = 0 if block == own[0] else None
                pltpu.matmul_acc_lhs(sums[unit * blocks + block], high[rows(unit, block)], load_staged_rhs=load)
                pltpu.matmul_acc_lhs(sums[unit * blocks + block], low[rows(unit, block)])
        for block in own:
            for unit in range(2):
                load = 1 if block == own[0] else None
                pltpu.matmul_acc_lhs(sums[unit * blocks + block], high[rows(unit, block)], load_staged_rhs=load)

    def first_product(section):
        for block in range(section * per_section, (section + 1) * per_section):
            for unit in range(2):
                place = rows(unit, block)
                other[0][place], other[1][place] = split(first_of(unit, block) * symbol_rows(unit, block, 1))

    def finish(stage, section, first=False):
        for block in range(section * per_section, (section + 1) * per_section):
            for unit in range(2):
                place = rows(unit, block)
                value = pltpu.matmul_pop(sums[unit * blocks + block])
                if stage == 0:
                    high, low = split(value * symbol_rows(unit, block, 1))
                    other[0][place], other[1][place] = high, low
                else:
                    start = start_of(unit, block)
                    held = start if first else state[place]
                    value = start + held * symbol_rows(unit, block, 0) + value
                    state[place] = value
                    now[0][place], now[1][place] = split(value)

    def sweep(last):
        order = ((0, 0), (0, 1), (1, 0), (1, 1))
        for index, unit in enumerate(order):
            if index + 1 < len(order):
                issue(*order[index + 1])
            elif not last:
                issue(*order[0])
            finish(*unit)
            if last and unit[0] == 1:
                done(unit[1])

    for section in range(2):
        first_product(section)
        issue(1, section)
    finish(1, 0, first=True)
    issue(0, 0)
    finish(1, 1, first=True)
    lax.fori_loop(0, count - 2, lambda _, carry: (sweep(False), carry)[1], 0)
    sweep(True)


def product_kernel(*refs):
    sources, step, both, out = refs[:-3], refs[-3], refs[-2], refs[-1]
    rows = sources[0].shape[0]
    for i, source in enumerate(sources):
        for first in range(0, rows, 2 * BLOCK):
            place = slice(first, first + 2 * BLOCK)
            value = source[place, :]
            target = slice(i * rows + first, i * rows + first + 2 * BLOCK)
            both[target, :] = value
            out[target, :] = dot_split(split(value), pair(step))


def unit_product(lhs, rhs, unit, sums):
    depth = lhs[0].shape[1]
    tile = sums.shape[1]
    for first in range(0, depth, tile):
        inner = slice(first, first + tile)
        for part in range(2):
            pltpu.matmul_push_rhs(rhs[part][inner], part, unit)
        pltpu.matmul_acc_lhs(sums, lhs[0][:, inner], load_staged_rhs=0)
        pltpu.matmul_acc_lhs(sums, lhs[1][:, inner])
        pltpu.matmul_acc_lhs(sums, lhs[0][:, inner], load_staged_rhs=1)
    return pltpu.matmul_pop(sums)


def apply_kernel(owners, mats, start, product, *refs):
    me = lax.axis_index("long")
    pieces, refs = refs[: len(owners)], refs[len(owners) :]
    table, steps, inverse, to_orders, out, coefficients, symbol, state, result, ready, *splits = refs
    now, other = splits[:2], splits[2:]
    columns, yord, _, order = out.shape
    lines = coefficients.shape[0]
    width = state.shape[1]
    rows = to_orders.shape[1] // 2
    half = state.shape[0] // 2
    factor = scale_of([mats[i] for i in range(NMAT)])[0, 0]

    for piece, ids in zip(pieces, owners):
        own = piece.shape[0] // len(ids)
        for index, distance in enumerate(ids):
            place = pl.multiple_of((me ^ distance) * own, own)
            coefficients[pl.ds(place, own), :] = piece[index * own : (index + 1) * own]
    values = split(coefficients[...])

    def all_symbols(*sums):
        for unit in range(2):
            columns_of = slice(unit * width, (unit + 1) * width)
            value = unit_product(values, (table.at[0, :, columns_of], table.at[1, :, columns_of]), unit, sums[unit])
            symbol[:, columns_of] = 0.5 - (0.5 * factor) * value

    pl.run_scoped(all_symbols, *[pltpu.ACC(unit)((lines, width), jnp.float32) for unit in range(2)])

    def start_of(unit, block):
        first = unit * half + block * BLOCK
        return start[first : first + BLOCK]

    def first_of(unit, block):
        first = unit * half + block * BLOCK
        return product[first : first + BLOCK]

    def to_panel(c, sums):
        place = slice(c * 2 * lines, (c + 1) * 2 * lines)
        unit = c * 2 * lines // half
        value = unit_product((to_orders[0], to_orders[1]), (now[0].at[place], now[1].at[place]), unit, sums[unit])
        value = split(value * factor)
        cosine, sine = (
            unit_product(
                value,
                tuple(inverse.at[part, :, unit * width : (unit + 1) * width] for part in range(2)),
                unit,
                sums[2 + unit],
            )
            for unit in range(2)
        )
        real = cosine[:rows] - sine[rows:]
        imag = cosine[rows:] + sine[:rows]
        for part, value in enumerate((real, imag)):
            for first in range(0, yord, lines):
                count = min(lines, yord - first)
                result[c, first : first + count, part, :] = value[:count, :order]
        pltpu.make_async_copy(result.at[c], out.at[c], ready.at[c]).start()

    early = columns % 4 == 0 and half + 4 * rows <= SUM_ROWS

    def run(*sums):
        blocks = 2 * (half // BLOCK)

        def done(section):
            if early:
                quarter = columns // 4
                for c in range(quarter):
                    for unit in range(2):
                        to_panel((2 * unit + section) * quarter + c, sums[blocks:])

        sweeps(2**NS_ITERS - 1, half, start_of, first_of, symbol, steps, state, now, other, sums[:blocks], done)

    sum_types = [pltpu.ACC(i % 2)((2 * rows, width), jnp.float32) for i in range(4)]
    block_types = [pltpu.ACC(unit)((BLOCK, width), jnp.float32) for unit in range(2) for _ in range(half // BLOCK)]
    pl.run_scoped(run, *block_types, *(sum_types if early else []))
    if not early:
        pl.run_scoped(lambda *sums: [to_panel(c, sums) for c in range(columns)] and None, *sum_types)
    for c in range(columns):
        pltpu.make_async_copy(result.at[c], out.at[c], ready.at[c]).wait()


SMEM = pl.BlockSpec(memory_space=pltpu.SMEM)
VMEM = pl.BlockSpec(memory_space=pltpu.VMEM)


def join_kernel(*refs):
    first = 0
    for piece in refs[:-1]:
        refs[-1][first : first + piece.shape[0], :] = piece[...]
        first += piece.shape[0]


def join(pieces):
    rows = sum(piece.shape[0] for piece in pieces)
    return pl.pallas_call(
        join_kernel,
        out_shape=jax.ShapeDtypeStruct((rows, pieces[0].shape[1]), jnp.float32),
        in_specs=[VMEM] * len(pieces),
        out_specs=VMEM,
        compiler_params=pltpu.CompilerParams(vmem_limit_bytes=4 * 2**20),
        cost_estimate=pl.CostEstimate(flops=0, bytes_accessed=8 * rows * pieces[0].shape[1], transcendentals=0),
        name="join",
    )(*pieces)


def local(pixel_map, materials, mode_panel):
    devices = lax.axis_size("long")
    own, npix = pixel_map.shape
    lines = own * devices
    columns, _, yord, order = mode_panel.shape
    width = up(order, LANES)
    kept = min(lines, yord)
    rows = up(kept, 16)
    groups = 2 if columns % 2 == 0 else 1
    share = columns // groups
    total = columns * 2 * lines
    limit = pltpu.CompilerParams(vmem_limit_bytes=4 * 2**20)

    inner, outer = pixel_tables(npix, order)
    mine = pl.pallas_call(
        coefficient_kernel,
        out_shape=jax.ShapeDtypeStruct((own, 2 * width), jnp.float32),
        in_specs=[SMEM] + [VMEM] * 3,
        out_specs=VMEM,
        compiler_params=pltpu.CompilerParams(vmem_limit_bytes=56 * 2**20),
        cost_estimate=pl.CostEstimate(flops=3 * 10**9, bytes_accessed=2**22, transcendentals=0),
        name="coefficient",
    )(materials, pixel_map, inner, outer)

    forward, inverse, step, back = order_tables(order, 1.0 / lines)
    to_lines, to_orders = line_tables(lines, yord, rows, kept)

    def exchange(block, distance):
        return lax.ppermute(block, "long", [(i, i ^ distance) for i in range(devices)])

    by_order = jnp.swapaxes(mode_panel, 1, 2)
    pieces, owners, starts = [mine], [(0,)], []
    distance = devices // 2
    while distance > 1:
        held = join(pieces) if len(pieces) > 1 else mine
        ids = tuple(d for piece in owners for d in piece)
        other = exchange(held, distance)
        if len(starts) < groups:
            group = len(starts)
            start = pl.pallas_call(
                spread_kernel,
                grid=(1,),
                out_shape=jax.ShapeDtypeStruct((share * 2 * lines, width), jnp.float32),
                in_specs=[pl.BlockSpec((share, yord, 2, order), lambda _, group=group: (group, 0, 0, 0)), VMEM, VMEM],
                out_specs=VMEM,
                scratch_shapes=[pltpu.VMEM((share, 2 * rows, width), jnp.float32)],
                compiler_params=limit,
                cost_estimate=pl.CostEstimate(flops=10**9, bytes_accessed=2**21, transcendentals=0),
                name="spread",
            )(by_order, forward, to_lines)
            start, other = lax.optimization_barrier((start, other))
            starts.append(start)
        if distance == 2:
            start, product = pl.pallas_call(
                product_kernel,
                out_shape=[jax.ShapeDtypeStruct((total, width), jnp.float32)] * 2,
                in_specs=[VMEM] * (groups + 1),
                out_specs=[VMEM] * 2,
                compiler_params=limit,
                cost_estimate=pl.CostEstimate(flops=10**9, bytes_accessed=2**21, transcendentals=0),
                name="product",
            )(*starts, step)
            start, product, other = lax.optimization_barrier((start, product, other))
            beside = exchange(held, 1)
            pieces = [held, beside, other, exchange(other, 1)]
            owners = [ids, tuple(d ^ 1 for d in ids), tuple(d ^ 2 for d in ids), tuple(d ^ 3 for d in ids)]
        else:
            pieces.append(other)
            owners.append(tuple(d ^ distance for d in ids))
        distance //= 2

    half = [pltpu.VMEM((total, width), jnp.bfloat16)]
    result = pl.pallas_call(
        functools.partial(apply_kernel, owners),
        out_shape=jax.ShapeDtypeStruct(by_order.shape, jnp.float32),
        in_specs=[SMEM] + [VMEM] * (6 + len(pieces)),
        out_specs=pl.BlockSpec(memory_space=pl.ANY),
        scratch_shapes=[
            pltpu.VMEM((lines, 2 * width), jnp.float32),
            pltpu.VMEM((lines, 2 * width), jnp.float32),
            pltpu.VMEM((total, width), jnp.float32),
            pltpu.VMEM(by_order.shape, jnp.float32),
            pltpu.SemaphoreType.DMA((columns,)),
        ]
        + half * 4,
        compiler_params=pltpu.CompilerParams(vmem_limit_bytes=10 * 2**20),
        cost_estimate=pl.CostEstimate(flops=1000000000, bytes_accessed=4194304, transcendentals=0),
        name="apply",
    )(
        materials,
        start,
        product,
        *pieces,
        symbol_table(order),
        np.concatenate([step, back]),
        inverse,
        to_orders,
    )
    return jnp.swapaxes(result, 1, 2)


def solution(mesh):
    in_specs = (P(("grp", "long"), None), P("grp"), P(("grp", "long"), None, None, None))
    out_specs = P(("grp", "long"), None, None, None)
    return jax.shard_map(local, mesh=mesh, in_specs=in_specs, out_specs=out_specs, check_vma=False)
```

```python
import functools
import math

import jax
import jax.numpy as jnp
import numpy as np
from jax import lax
from jax.experimental import pallas as pl
from jax.experimental.pallas import tpu as pltpu
from jax.sharding import PartitionSpec as P

NMAT = 4
NS_ITERS = 3
LANES = 128
BLOCK = 128


def up(value, step):
    return -(-value // step) * step


def split(x):
    high = x.astype(jnp.bfloat16)
    low = (x - high.astype(jnp.float32)).astype(jnp.bfloat16)
    return high, low


def dot(a, b):
    return jnp.dot(a, b, preferred_element_type=jnp.float32)


def dot_split(a, b):
    return dot(a[0], b[0]) + dot(a[1], b[0]) + dot(a[0], b[1])


def split_table(table):
    table = np.asarray(table, np.float32)
    high = table.astype(jnp.bfloat16)
    low = (table - high.astype(np.float32)).astype(jnp.bfloat16)
    return np.stack([high, low])


def turn(product, period):
    return np.mod(product, period) * (2.0 * math.pi / period)


def pixel_tables(npix, order):
    width = up(order, LANES)
    k = np.arange(order)
    inner = np.zeros((LANES, 2 * width))
    angle = turn(np.arange(LANES)[:, None] * k[None, :], npix)
    inner[:, :order] = np.cos(angle) / npix
    inner[:, width : width + order] = np.sin(angle) / npix
    chunks = npix // LANES
    outer = np.zeros((chunks, 2 * width), np.float32)
    angle = turn(LANES * np.arange(chunks)[:, None] * k[None, :], npix)
    outer[:, :order] = np.cos(angle)
    outer[:, width : width + order] = np.sin(angle)
    return split_table(inner), outer


def symbol_table(order):
    width = up(order, LANES)
    k = np.arange(order)
    weight = np.where(k == 0, 1.0, 2.0)[:, None]
    table = np.zeros((2 * width, 2 * width))
    for half in range(2):
        angle = turn(k[:, None] * (2 * np.arange(order)[None, :] + half), 2 * order)
        columns = slice(half * width, half * width + order)
        table[:order, columns] = weight * np.cos(angle)
        table[width : width + order, columns] = weight * np.sin(angle)
    return split_table(table)


def order_tables(order, scale):
    width = up(order, LANES)
    centred = np.arange(order) - (order - 1) // 2
    whole = 2 * np.arange(order)
    angle = turn(centred[:, None] * whole[None, :], 2 * order)
    forward = np.zeros((width, 2 * width))
    forward[:order, :order] = np.cos(angle)
    forward[:order, width : width + order] = np.sin(angle)
    inverse = np.zeros((width, 2 * width))
    inverse[:order, :order] = np.cos(angle).T * (scale / order)
    inverse[:order, width : width + order] = np.sin(angle).T * (scale / order)
    gap = whole[:, None] - (whole + 1)[None, :]
    angle = turn(centred[:, None, None] * gap[None], 2 * order)
    step = np.zeros((width, width))
    step[:order, :order] = np.cos(angle).sum(0) / order
    return split_table(forward), split_table(inverse), split_table(step), split_table(step.T)


def line_tables(lines, yord, rows, kept):
    half = (yord - 1) // 2
    angle = turn(np.arange(lines)[:, None] * (np.arange(kept) - half)[None, :], lines)
    cosine, sine = np.zeros((lines, rows)), np.zeros((lines, rows))
    cosine[:, :kept], sine[:, :kept] = np.cos(angle), np.sin(angle)
    spread = np.block([[cosine, -sine], [sine, cosine]])
    return split_table(spread), split_table(spread.T)


def scale_of(materials):
    low = functools.reduce(jnp.minimum, materials)
    high = functools.reduce(jnp.maximum, materials)
    full = lambda value: jnp.full((1, LANES), value, jnp.float32)
    return 2.0 / (1.0 / full(low) + 1.0 / full(high))


def coefficient_kernel(mats, pixels, inner, outer, out):
    inverse = [1.0 / jnp.full((1, LANES), mats[i], jnp.float32) for i in range(NMAT)]
    lines, npix = pixels.shape
    width = outer.shape[1] // 2
    chunks = npix // LANES
    parts = []
    for chunk in range(chunks):
        index = pixels[:, chunk * LANES : (chunk + 1) * LANES]
        value = jnp.zeros((lines, LANES), jnp.float32)
        for i in range(NMAT):
            value = value + jnp.where(index == i, inverse[i], 0.0)
        parts.append(value)
    inside = dot_split(split(jnp.concatenate(parts, 0)), (inner[0], inner[1]))
    real = jnp.zeros((lines, width), jnp.float32)
    imag = jnp.zeros((lines, width), jnp.float32)
    for chunk in range(chunks):
        rows = slice(chunk * lines, (chunk + 1) * lines)
        in_cos, in_sin = inside[rows, :width], inside[rows, width:]
        out_cos, out_sin = outer[chunk : chunk + 1, :width], outer[chunk : chunk + 1, width:]
        real = real + in_cos * out_cos - in_sin * out_sin
        imag = imag - in_cos * out_sin - in_sin * out_cos
    out[:, :width] = real
    out[:, width:] = imag


def pair(ref):
    return ref[0], ref[1]


def spread_kernel(panel, forward, to_lines, out, folded):
    _, yord, _, order = panel.shape
    width = out.shape[1]
    rows = folded.shape[1] // 2
    double_lines = to_lines.shape[1]
    lines = double_lines // 2
    kept = min(lines, yord)
    for c in range(folded.shape[0]):
        folded[c] = jnp.zeros((2 * rows, width), jnp.float32)
        for part in range(2):
            base = part * rows
            folded[c, base : base + kept, :order] = panel[c, :kept, part, :]
            for first in range(lines, yord, lines):
                count = min(lines, yord - first)
                folded[c, base : base + count, :order] += panel[c, first : first + count, part, :]
        both = dot_split(split(folded[c]), pair(forward))
        cosine, sine = both[:, :width], both[:, width:]
        real = cosine[:rows] + sine[rows:]
        imag = cosine[rows:] - sine[:rows]
        high, low = split(jnp.concatenate([real, imag], 0))
        value = dot(to_lines[0], high) + dot(to_lines[1], high) + dot(to_lines[0], low)
        out[c * double_lines : (c + 1) * double_lines, :] = value


def sweeps(count, half, start_of, first_of, symbol, steps, state, now, other, sums):
    lines, width = symbol.shape[0], state.shape[1]
    blocks = half // BLOCK
    per_section = blocks // 2

    def rows(unit, block):
        return slice(unit * half + block * BLOCK, unit * half + (block + 1) * BLOCK)

    def symbol_rows(unit, block, part):
        first = (unit * half + block * BLOCK) % lines
        return symbol[first : first + BLOCK, part * width : (part + 1) * width]

    def issue(stage, section):
        high, low = now if stage == 0 else other
        own = range(section * per_section, (section + 1) * per_section)
        for unit in range(2):
            for part in range(2):
                pltpu.matmul_push_rhs(steps[2 * stage + part], part, unit)
        for block in own:
            for unit in range(2):
                load = 0 if block == own[0] else None
                pltpu.matmul_acc_lhs(sums[unit * blocks + block], high[rows(unit, block)], load_staged_rhs=load)
                pltpu.matmul_acc_lhs(sums[unit * blocks + block], low[rows(unit, block)])
        for block in own:
            for unit in range(2):
                load = 1 if block == own[0] else None
                pltpu.matmul_acc_lhs(sums[unit * blocks + block], high[rows(unit, block)], load_staged_rhs=load)

    def first_product(section):
        for block in range(section * per_section, (section + 1) * per_section):
            for unit in range(2):
                place = rows(unit, block)
                other[0][place], other[1][place] = split(first_of(unit, block) * symbol_rows(unit, block, 1))
                state[place] = start_of(unit, block)

    def finish(stage, section):
        for block in range(section * per_section, (section + 1) * per_section):
            for unit in range(2):
                place = rows(unit, block)
                value = pltpu.matmul_pop(sums[unit * blocks + block])
                if stage == 0:
                    high, low = split(value * symbol_rows(unit, block, 1))
                    other[0][place], other[1][place] = high, low
                else:
                    value = start_of(unit, block) + state[place] * symbol_rows(unit, block, 0) + value
                    state[place] = value
                    now[0][place], now[1][place] = split(value)

    def body(_, carry):
        issue(0, 0)
        finish(1, 1)
        issue(0, 1)
        finish(0, 0)
        issue(1, 0)
        finish(0, 1)
        issue(1, 1)
        finish(1, 0)
        return carry

    for section in range(2):
        first_product(section)
        issue(1, section)
    finish(1, 0)
    lax.fori_loop(0, count - 1, body, 0)
    finish(1, 1)


def product_kernel(*refs):
    sources, step, both, out = refs[:-3], refs[-3], refs[-2], refs[-1]
    rows = sources[0].shape[0]
    for i, source in enumerate(sources):
        for first in range(0, rows, 2 * BLOCK):
            place = slice(first, first + 2 * BLOCK)
            value = source[place, :]
            target = slice(i * rows + first, i * rows + first + 2 * BLOCK)
            both[target, :] = value
            out[target, :] = dot_split(split(value), pair(step))


def unit_issue(lhs, rhs, unit, sums):
    depth = lhs[0].shape[1]
    tile = sums.shape[1]
    for first in range(0, depth, tile):
        inner = slice(first, first + tile)
        for part in range(2):
            pltpu.matmul_push_rhs(rhs[part][inner], part, unit)
        pltpu.matmul_acc_lhs(sums, lhs[0][:, inner], load_staged_rhs=0)
        pltpu.matmul_acc_lhs(sums, lhs[1][:, inner])
        pltpu.matmul_acc_lhs(sums, lhs[0][:, inner], load_staged_rhs=1)


def unit_product(lhs, rhs, unit, sums):
    unit_issue(lhs, rhs, unit, sums)
    return pltpu.matmul_pop(sums)


def apply_kernel(owners, mats, start, product, *refs):
    me = lax.axis_index("long")
    pieces, refs = refs[: len(owners)], refs[len(owners) :]
    table, steps, inverse, to_orders, out, coefficients, symbol, state, result, ready, *splits = refs
    now, other = splits[:2], splits[2:]
    columns, yord, _, order = out.shape
    lines = coefficients.shape[0]
    width = state.shape[1]
    rows = to_orders.shape[1] // 2
    half = state.shape[0] // 2
    factor = scale_of([mats[i] for i in range(NMAT)])[0, 0]

    for piece, ids in zip(pieces, owners):
        own = piece.shape[0] // len(ids)
        for index, distance in enumerate(ids):
            place = pl.multiple_of((me ^ distance) * own, own)
            coefficients[pl.ds(place, own), :] = piece[index * own : (index + 1) * own]
    values = split(coefficients[...])

    def all_symbols(*sums):
        for unit in range(2):
            columns_of = slice(unit * width, (unit + 1) * width)
            value = unit_product(values, (table.at[0, :, columns_of], table.at[1, :, columns_of]), unit, sums[unit])
            symbol[:, columns_of] = 0.5 - (0.5 * factor) * value

    pl.run_scoped(all_symbols, *[pltpu.ACC(unit)((lines, width), jnp.float32) for unit in range(2)])

    def start_of(unit, block):
        first = unit * half + block * BLOCK
        return start[first : first + BLOCK]

    def first_of(unit, block):
        first = unit * half + block * BLOCK
        return product[first : first + BLOCK]

    def run(*sums):
        sweeps(2**NS_ITERS - 1, half, start_of, first_of, symbol, steps, state, now, other, sums)

    pl.run_scoped(run, *[pltpu.ACC(unit)((BLOCK, width), jnp.float32) for unit in range(2) for _ in range(half // BLOCK)])

    def copy_out(c):
        return pltpu.make_async_copy(result.at[c], out.at[c], ready.at[c])

    unit_of = [c * 2 * lines // half if columns > 1 else 0 for c in range(columns)]
    order_of = sorted(range(columns), key=lambda c: (c % max(columns // 2, 1), c))
    buffers = min(2, columns)

    def all_columns(*sums):
        in_orders, in_panel = sums[:columns], sums[columns:]

        def transform(index):
            c = order_of[index]
            value = split(pltpu.matmul_pop(in_orders[c]) * factor)
            for side in range(2):
                table_of = tuple(inverse.at[part, :, side * width : (side + 1) * width] for part in range(2))
                unit_issue(value, table_of, side, in_panel[2 * (index % buffers) + side])

        def leave(index):
            c = order_of[index]
            cosine, sine = (pltpu.matmul_pop(in_panel[2 * (index % buffers) + side]) for side in range(2))
            real = cosine[:rows] - sine[rows:]
            imag = cosine[rows:] + sine[:rows]
            for part, value in enumerate((real, imag)):
                for first in range(0, yord, lines):
                    count = min(lines, yord - first)
                    result[c, first : first + count, part, :] = value[:count, :order]
            copy_out(c).start()

        for c in order_of:
            place = slice(c * 2 * lines, (c + 1) * 2 * lines)
            unit_issue((to_orders[0], to_orders[1]), (now[0].at[place], now[1].at[place]), unit_of[c], in_orders[c])
        for index in range(columns):
            transform(index)
            if index + 1 >= buffers:
                leave(index + 1 - buffers)
        for index in range(columns + 1 - buffers, columns):
            leave(index)

    column_sums = [pltpu.ACC(unit)((2 * rows, width), jnp.float32) for unit in unit_of]
    panel_sums = [pltpu.ACC(i % 2)((2 * rows, width), jnp.float32) for i in range(2 * buffers)]
    pl.run_scoped(all_columns, *column_sums, *panel_sums)
    for c in range(columns):
        copy_out(c).wait()


SMEM = pl.BlockSpec(memory_space=pltpu.SMEM)
VMEM = pl.BlockSpec(memory_space=pltpu.VMEM)


def join_kernel(*refs):
    first = 0
    for piece in refs[:-1]:
        refs[-1][first : first + piece.shape[0], :] = piece[...]
        first += piece.shape[0]


def join(pieces):
    rows = sum(piece.shape[0] for piece in pieces)
    return pl.pallas_call(
        join_kernel,
        out_shape=jax.ShapeDtypeStruct((rows, pieces[0].shape[1]), jnp.float32),
        in_specs=[VMEM] * len(pieces),
        out_specs=VMEM,
        compiler_params=pltpu.CompilerParams(vmem_limit_bytes=4 * 2**20),
        cost_estimate=pl.CostEstimate(flops=0, bytes_accessed=8 * rows * pieces[0].shape[1], transcendentals=0),
        name="join",
    )(*pieces)


def local(pixel_map, materials, mode_panel):
    devices = lax.axis_size("long")
    own, npix = pixel_map.shape
    lines = own * devices
    columns, _, yord, order = mode_panel.shape
    width = up(order, LANES)
    kept = min(lines, yord)
    rows = up(kept, 16)
    groups = 2 if columns % 2 == 0 else 1
    share = columns // groups
    total = columns * 2 * lines
    limit = pltpu.CompilerParams(vmem_limit_bytes=4 * 2**20)

    inner, outer = pixel_tables(npix, order)
    mine = pl.pallas_call(
        coefficient_kernel,
        out_shape=jax.ShapeDtypeStruct((own, 2 * width), jnp.float32),
        in_specs=[SMEM] + [VMEM] * 3,
        out_specs=VMEM,
        compiler_params=pltpu.CompilerParams(vmem_limit_bytes=56 * 2**20),
        cost_estimate=pl.CostEstimate(flops=3 * 10**9, bytes_accessed=2**22, transcendentals=0),
        name="coefficient",
    )(materials, pixel_map, inner, outer)

    forward, inverse, step, back = order_tables(order, 1.0 / lines)
    to_lines, to_orders = line_tables(lines, yord, rows, kept)

    def exchange(block, distance):
        return lax.ppermute(block, "long", [(i, i ^ distance) for i in range(devices)])

    by_order = jnp.swapaxes(mode_panel, 1, 2)
    pieces, owners, starts = [mine], [(0,)], []
    distance = devices // 2
    while distance > 1:
        held = join(pieces) if len(pieces) > 1 else mine
        ids = tuple(d for piece in owners for d in piece)
        other = exchange(held, distance)
        if len(starts) < groups:
            group = len(starts)
            start = pl.pallas_call(
                spread_kernel,
                grid=(1,),
                out_shape=jax.ShapeDtypeStruct((share * 2 * lines, width), jnp.float32),
                in_specs=[pl.BlockSpec((share, yord, 2, order), lambda _, group=group: (group, 0, 0, 0)), VMEM, VMEM],
                out_specs=VMEM,
                scratch_shapes=[pltpu.VMEM((share, 2 * rows, width), jnp.float32)],
                compiler_params=limit,
                cost_estimate=pl.CostEstimate(flops=10**9, bytes_accessed=2**21, transcendentals=0),
                name="spread",
            )(by_order, forward, to_lines)
            start, other = lax.optimization_barrier((start, other))
            starts.append(start)
        if distance == 2:
            start, product = pl.pallas_call(
                product_kernel,
                out_shape=[jax.ShapeDtypeStruct((total, width), jnp.float32)] * 2,
                in_specs=[VMEM] * (groups + 1),
                out_specs=[VMEM] * 2,
                compiler_params=limit,
                cost_estimate=pl.CostEstimate(flops=10**9, bytes_accessed=2**21, transcendentals=0),
                name="product",
            )(*starts, step)
            start, product, other = lax.optimization_barrier((start, product, other))
            beside = exchange(held, 1)
            pieces = [held, beside, other, exchange(other, 1)]
            owners = [ids, tuple(d ^ 1 for d in ids), tuple(d ^ 2 for d in ids), tuple(d ^ 3 for d in ids)]
        else:
            pieces.append(other)
            owners.append(tuple(d ^ distance for d in ids))
        distance //= 2

    half = [pltpu.VMEM((total, width), jnp.bfloat16)]
    result = pl.pallas_call(
        functools.partial(apply_kernel, owners),
        out_shape=jax.ShapeDtypeStruct(by_order.shape, jnp.float32),
        in_specs=[SMEM] + [VMEM] * (6 + len(pieces)),
        out_specs=pl.BlockSpec(memory_space=pl.ANY),
        scratch_shapes=[
            pltpu.VMEM((lines, 2 * width), jnp.float32),
            pltpu.VMEM((lines, 2 * width), jnp.float32),
            pltpu.VMEM((total, width), jnp.float32),
            pltpu.VMEM(by_order.shape, jnp.float32),
            pltpu.SemaphoreType.DMA((columns,)),
        ]
        + half * 4,
        compiler_params=pltpu.CompilerParams(vmem_limit_bytes=10 * 2**20),
        cost_estimate=pl.CostEstimate(flops=1000000000, bytes_accessed=4194304, transcendentals=0),
        name="apply",
    )(
        materials,
        start,
        product,
        *pieces,
        symbol_table(order),
        np.concatenate([step, back]),
        inverse,
        to_orders,
    )
    return jnp.swapaxes(result, 1, 2)


def solution(mesh):
    in_specs = (P(("grp", "long"), None), P("grp"), P(("grp", "long"), None, None, None))
    out_specs = P(("grp", "long"), None, None, None)
    return jax.shard_map(local, mesh=mesh, in_specs=in_specs, out_specs=out_specs, check_vma=False)
```

```python
import functools
import math

import jax
import jax.numpy as jnp
import numpy as np
from jax import lax
from jax.experimental import pallas as pl
from jax.experimental.pallas import tpu as pltpu
from jax.sharding import PartitionSpec as P

NMAT = 4
NS_ITERS = 3
LANES = 128
BLOCK = 128


def up(value, step):
    return -(-value // step) * step


def split(x):
    high = x.astype(jnp.bfloat16)
    low = (x - high.astype(jnp.float32)).astype(jnp.bfloat16)
    return high, low


def dot(a, b):
    return jnp.dot(a, b, preferred_element_type=jnp.float32)


def dot_split(a, b):
    return dot(a[0], b[0]) + dot(a[1], b[0]) + dot(a[0], b[1])


def split_table(table):
    table = np.asarray(table, np.float32)
    high = table.astype(jnp.bfloat16)
    low = (table - high.astype(np.float32)).astype(jnp.bfloat16)
    return np.stack([high, low])


def turn(product, period):
    return np.mod(product, period) * (2.0 * math.pi / period)


def pixel_tables(npix, order):
    width = up(order, LANES)
    k = np.arange(order)
    inner = np.zeros((LANES, 2 * width))
    angle = turn(np.arange(LANES)[:, None] * k[None, :], npix)
    inner[:, :order] = np.cos(angle) / npix
    inner[:, width : width + order] = np.sin(angle) / npix
    chunks = npix // LANES
    outer = np.zeros((chunks, 2 * width), np.float32)
    angle = turn(LANES * np.arange(chunks)[:, None] * k[None, :], npix)
    outer[:, :order] = np.cos(angle)
    outer[:, width : width + order] = np.sin(angle)
    return split_table(inner), outer


def symbol_table(order):
    width = up(order, LANES)
    k = np.arange(order)
    weight = np.where(k == 0, 1.0, 2.0)[:, None]
    table = np.zeros((2 * width, 2 * width))
    for half in range(2):
        angle = turn(k[:, None] * (2 * np.arange(order)[None, :] + half), 2 * order)
        columns = slice(half * width, half * width + order)
        table[:order, columns] = weight * np.cos(angle)
        table[width : width + order, columns] = weight * np.sin(angle)
    return split_table(table)


def order_tables(order, scale):
    width = up(order, LANES)
    centred = np.arange(order) - (order - 1) // 2
    whole = 2 * np.arange(order)
    angle = turn(centred[:, None] * whole[None, :], 2 * order)
    forward = np.zeros((width, 2 * width))
    forward[:order, :order] = np.cos(angle)
    forward[:order, width : width + order] = np.sin(angle)
    inverse = np.zeros((width, 2 * width))
    inverse[:order, :order] = np.cos(angle).T * (scale / order)
    inverse[:order, width : width + order] = np.sin(angle).T * (scale / order)
    gap = whole[:, None] - (whole + 1)[None, :]
    angle = turn(centred[:, None, None] * gap[None], 2 * order)
    step = np.zeros((width, width))
    step[:order, :order] = np.cos(angle).sum(0) / order
    return split_table(forward), split_table(inverse), split_table(step), split_table(step.T)


def line_tables(lines, yord, rows, kept):
    half = (yord - 1) // 2
    angle = turn(np.arange(lines)[:, None] * (np.arange(kept) - half)[None, :], lines)
    cosine, sine = np.zeros((lines, rows)), np.zeros((lines, rows))
    cosine[:, :kept], sine[:, :kept] = np.cos(angle), np.sin(angle)
    spread = np.block([[cosine, -sine], [sine, cosine]])
    return split_table(spread), split_table(spread.T)


def scale_of(materials):
    low = functools.reduce(jnp.minimum, materials)
    high = functools.reduce(jnp.maximum, materials)
    full = lambda value: jnp.full((1, LANES), value, jnp.float32)
    return 2.0 / (1.0 / full(low) + 1.0 / full(high))


def coefficient_kernel(mats, pixels, inner, outer, out):
    inverse = [1.0 / jnp.full((1, LANES), mats[i], jnp.float32) for i in range(NMAT)]
    lines, npix = pixels.shape
    width = outer.shape[1] // 2
    chunks = npix // LANES
    parts = []
    for chunk in range(chunks):
        index = pixels[:, chunk * LANES : (chunk + 1) * LANES]
        value = jnp.zeros((lines, LANES), jnp.float32)
        for i in range(NMAT):
            value = value + jnp.where(index == i, inverse[i], 0.0)
        parts.append(value)
    inside = dot_split(split(jnp.concatenate(parts, 0)), (inner[0], inner[1]))
    real = jnp.zeros((lines, width), jnp.float32)
    imag = jnp.zeros((lines, width), jnp.float32)
    for chunk in range(chunks):
        rows = slice(chunk * lines, (chunk + 1) * lines)
        in_cos, in_sin = inside[rows, :width], inside[rows, width:]
        out_cos, out_sin = outer[chunk : chunk + 1, :width], outer[chunk : chunk + 1, width:]
        real = real + in_cos * out_cos - in_sin * out_sin
        imag = imag - in_cos * out_sin - in_sin * out_cos
    out[:, :width] = real
    out[:, width:] = imag


def pair(ref):
    return ref[0], ref[1]


def spread_kernel(panel, forward, to_lines, out, folded):
    _, yord, _, order = panel.shape
    width = out.shape[1]
    rows = folded.shape[1] // 2
    double_lines = to_lines.shape[1]
    lines = double_lines // 2
    kept = min(lines, yord)
    for c in range(folded.shape[0]):
        folded[c] = jnp.zeros((2 * rows, width), jnp.float32)
        for part in range(2):
            base = part * rows
            folded[c, base : base + kept, :order] = panel[c, :kept, part, :]
            for first in range(lines, yord, lines):
                count = min(lines, yord - first)
                folded[c, base : base + count, :order] += panel[c, first : first + count, part, :]
        both = dot_split(split(folded[c]), pair(forward))
        cosine, sine = both[:, :width], both[:, width:]
        real = cosine[:rows] + sine[rows:]
        imag = cosine[rows:] - sine[:rows]
        high, low = split(jnp.concatenate([real, imag], 0))
        value = dot(to_lines[0], high) + dot(to_lines[1], high) + dot(to_lines[0], low)
        out[c * double_lines : (c + 1) * double_lines, :] = value


def sweeps(count, half, start_of, first_of, symbol, steps, state, now, other, sums):
    lines, width = symbol.shape[0], state.shape[1]
    blocks = half // BLOCK
    per_section = blocks // 2

    def rows(unit, block):
        return slice(unit * half + block * BLOCK, unit * half + (block + 1) * BLOCK)

    def symbol_rows(unit, block, part):
        first = (unit * half + block * BLOCK) % lines
        return symbol[first : first + BLOCK, part * width : (part + 1) * width]

    def issue(stage, section):
        high, low = now if stage == 0 else other
        own = range(section * per_section, (section + 1) * per_section)
        for unit in range(2):
            for part in range(2):
                pltpu.matmul_push_rhs(steps[2 * stage + part], part, unit)
        for block in own:
            for unit in range(2):
                load = 0 if block == own[0] else None
                pltpu.matmul_acc_lhs(sums[unit * blocks + block], high[rows(unit, block)], load_staged_rhs=load)
                pltpu.matmul_acc_lhs(sums[unit * blocks + block], low[rows(unit, block)])
        for block in own:
            for unit in range(2):
                load = 1 if block == own[0] else None
                pltpu.matmul_acc_lhs(sums[unit * blocks + block], high[rows(unit, block)], load_staged_rhs=load)

    def first_product(section):
        for block in range(section * per_section, (section + 1) * per_section):
            for unit in range(2):
                place = rows(unit, block)
                other[0][place], other[1][place] = split(first_of(unit, block) * symbol_rows(unit, block, 1))
                state[place] = start_of(unit, block)

    def finish(stage, section):
        for block in range(section * per_section, (section + 1) * per_section):
            for unit in range(2):
                place = rows(unit, block)
                value = pltpu.matmul_pop(sums[unit * blocks + block])
                if stage == 0:
                    high, low = split(value * symbol_rows(unit, block, 1))
                    other[0][place], other[1][place] = high, low
                else:
                    value = start_of(unit, block) + state[place] * symbol_rows(unit, block, 0) + value
                    state[place] = value
                    now[0][place], now[1][place] = split(value)

    def body(_, carry):
        issue(0, 0)
        finish(1, 1)
        issue(0, 1)
        finish(0, 0)
        issue(1, 0)
        finish(0, 1)
        issue(1, 1)
        finish(1, 0)
        return carry

    for section in range(2):
        first_product(section)
        issue(1, section)
    finish(1, 0)
    lax.fori_loop(0, count - 1, body, 0)
    finish(1, 1)


def symbol_kernel(mats, *refs):
    pieces, table, out = refs[:-2], refs[-2], refs[-1]
    factor = scale_of([mats[i] for i in range(NMAT)])[0, 0]
    values = jnp.concatenate([piece[...] for piece in pieces], 0)
    out[...] = 0.5 - (0.5 * factor) * dot_split(split(values), pair(table))


def product_kernel(*refs):
    sources, step, both, out = refs[:-3], refs[-3], refs[-2], refs[-1]
    rows = sources[0].shape[0]
    for i, source in enumerate(sources):
        for first in range(0, rows, 2 * BLOCK):
            place = slice(first, first + 2 * BLOCK)
            value = source[place, :]
            target = slice(i * rows + first, i * rows + first + 2 * BLOCK)
            both[target, :] = value
            out[target, :] = dot_split(split(value), pair(step))


def unit_issue(lhs, rhs, unit, sums):
    depth = lhs[0].shape[1]
    tile = sums.shape[1]
    for first in range(0, depth, tile):
        inner = slice(first, first + tile)
        for part in range(2):
            pltpu.matmul_push_rhs(rhs[part][inner], part, unit)
        pltpu.matmul_acc_lhs(sums, lhs[0][:, inner], load_staged_rhs=0)
        pltpu.matmul_acc_lhs(sums, lhs[1][:, inner])
        pltpu.matmul_acc_lhs(sums, lhs[0][:, inner], load_staged_rhs=1)


def unit_product(lhs, rhs, unit, sums):
    unit_issue(lhs, rhs, unit, sums)
    return pltpu.matmul_pop(sums)


def apply_kernel(owners, mats, start, product, early, last, *refs):
    me = lax.axis_index("long")
    table, steps, inverse, to_orders, out, symbol, state, result, ready, *splits = refs
    now, other = splits[:2], splits[2:]
    columns, yord, _, order = out.shape
    lines = symbol.shape[0]
    width = state.shape[1]
    rows = to_orders.shape[1] // 2
    half = state.shape[0] // 2
    factor = scale_of([mats[i] for i in range(NMAT)])[0, 0]

    def place_of(distance, own):
        return pl.ds(pl.multiple_of((me ^ distance) * own, own), own)

    own = last.shape[0] // len(owners[-1])
    values = split(last[...])

    def last_symbols(*sums):
        for unit in range(2):
            columns_of = slice(unit * width, (unit + 1) * width)
            value = unit_product(values, (table.at[0, :, columns_of], table.at[1, :, columns_of]), unit, sums[unit])
            value = 0.5 - (0.5 * factor) * value
            for index, distance in enumerate(owners[-1]):
                symbol[place_of(distance, own), columns_of] = value[index * own : (index + 1) * own]

    for index, distance in enumerate(d for ids in owners[:-1] for d in ids):
        symbol[place_of(distance, own), :] = early[index * own : (index + 1) * own, :]
    pl.run_scoped(last_symbols, *[pltpu.ACC(unit)((last.shape[0], width), jnp.float32) for unit in range(2)])

    def start_of(unit, block):
        first = unit * half + block * BLOCK
        return start[first : first + BLOCK]

    def first_of(unit, block):
        first = unit * half + block * BLOCK
        return product[first : first + BLOCK]

    def run(*sums):
        sweeps(2**NS_ITERS - 1, half, start_of, first_of, symbol, steps, state, now, other, sums)

    pl.run_scoped(run, *[pltpu.ACC(unit)((BLOCK, width), jnp.float32) for unit in range(2) for _ in range(half // BLOCK)])

    def copy_out(c):
        return pltpu.make_async_copy(result.at[c], out.at[c], ready.at[c])

    unit_of = [c * 2 * lines // half if columns > 1 else 0 for c in range(columns)]
    order_of = sorted(range(columns), key=lambda c: (c % max(columns // 2, 1), c))
    buffers = min(2, columns)

    def all_columns(*sums):
        in_orders, in_panel = sums[:columns], sums[columns:]

        def transform(index):
            c = order_of[index]
            value = split(pltpu.matmul_pop(in_orders[c]) * factor)
            for side in range(2):
                table_of = tuple(inverse.at[part, :, side * width : (side + 1) * width] for part in range(2))
                unit_issue(value, table_of, side, in_panel[2 * (index % buffers) + side])

        def leave(index):
            c = order_of[index]
            cosine, sine = (pltpu.matmul_pop(in_panel[2 * (index % buffers) + side]) for side in range(2))
            real = cosine[:rows] - sine[rows:]
            imag = cosine[rows:] + sine[:rows]
            for part, value in enumerate((real, imag)):
                for first in range(0, yord, lines):
                    count = min(lines, yord - first)
                    result[c, first : first + count, part, :] = value[:count, :order]
            copy_out(c).start()

        for c in order_of:
            place = slice(c * 2 * lines, (c + 1) * 2 * lines)
            unit_issue((to_orders[0], to_orders[1]), (now[0].at[place], now[1].at[place]), unit_of[c], in_orders[c])
        for index in range(columns):
            transform(index)
            if index + 1 >= buffers:
                leave(index + 1 - buffers)
        for index in range(columns + 1 - buffers, columns):
            leave(index)

    column_sums = [pltpu.ACC(unit)((2 * rows, width), jnp.float32) for unit in unit_of]
    panel_sums = [pltpu.ACC(i % 2)((2 * rows, width), jnp.float32) for i in range(2 * buffers)]
    pl.run_scoped(all_columns, *column_sums, *panel_sums)
    for c in range(columns):
        copy_out(c).wait()


SMEM = pl.BlockSpec(memory_space=pltpu.SMEM)
VMEM = pl.BlockSpec(memory_space=pltpu.VMEM)


def join_kernel(*refs):
    first = 0
    for piece in refs[:-1]:
        refs[-1][first : first + piece.shape[0], :] = piece[...]
        first += piece.shape[0]


def join(pieces):
    rows = sum(piece.shape[0] for piece in pieces)
    return pl.pallas_call(
        join_kernel,
        out_shape=jax.ShapeDtypeStruct((rows, pieces[0].shape[1]), jnp.float32),
        in_specs=[VMEM] * len(pieces),
        out_specs=VMEM,
        compiler_params=pltpu.CompilerParams(vmem_limit_bytes=4 * 2**20),
        cost_estimate=pl.CostEstimate(flops=0, bytes_accessed=8 * rows * pieces[0].shape[1], transcendentals=0),
        name="join",
    )(*pieces)


def local(pixel_map, materials, mode_panel):
    devices = lax.axis_size("long")
    own, npix = pixel_map.shape
    lines = own * devices
    columns, _, yord, order = mode_panel.shape
    width = up(order, LANES)
    kept = min(lines, yord)
    rows = up(kept, 16)
    groups = 2 if columns % 2 == 0 else 1
    share = columns // groups
    total = columns * 2 * lines
    limit = pltpu.CompilerParams(vmem_limit_bytes=4 * 2**20)

    inner, outer = pixel_tables(npix, order)
    mine = pl.pallas_call(
        coefficient_kernel,
        out_shape=jax.ShapeDtypeStruct((own, 2 * width), jnp.float32),
        in_specs=[SMEM] + [VMEM] * 3,
        out_specs=VMEM,
        compiler_params=pltpu.CompilerParams(vmem_limit_bytes=56 * 2**20),
        cost_estimate=pl.CostEstimate(flops=3 * 10**9, bytes_accessed=2**22, transcendentals=0),
        name="coefficient",
    )(materials, pixel_map, inner, outer)

    forward, inverse, step, back = order_tables(order, 1.0 / lines)
    to_lines, to_orders = line_tables(lines, yord, rows, kept)

    def exchange(block, distance):
        return lax.ppermute(block, "long", [(i, i ^ distance) for i in range(devices)])

    by_order = jnp.swapaxes(mode_panel, 1, 2)
    pieces, owners, starts = [mine], [(0,)], []
    distance = devices // 2
    while distance > 1:
        held = join(pieces) if len(pieces) > 1 else mine
        ids = tuple(d for piece in owners for d in piece)
        other = exchange(held, distance)
        if len(starts) < groups:
            group = len(starts)
            start = pl.pallas_call(
                spread_kernel,
                grid=(1,),
                out_shape=jax.ShapeDtypeStruct((share * 2 * lines, width), jnp.float32),
                in_specs=[pl.BlockSpec((share, yord, 2, order), lambda _, group=group: (group, 0, 0, 0)), VMEM, VMEM],
                out_specs=VMEM,
                scratch_shapes=[pltpu.VMEM((share, 2 * rows, width), jnp.float32)],
                compiler_params=limit,
                cost_estimate=pl.CostEstimate(flops=10**9, bytes_accessed=2**21, transcendentals=0),
                name="spread",
            )(by_order, forward, to_lines)
            start, other = lax.optimization_barrier((start, other))
            starts.append(start)
        if distance == 2:
            start, product = pl.pallas_call(
                product_kernel,
                out_shape=[jax.ShapeDtypeStruct((total, width), jnp.float32)] * 2,
                in_specs=[VMEM] * (groups + 1),
                out_specs=[VMEM] * 2,
                compiler_params=limit,
                cost_estimate=pl.CostEstimate(flops=10**9, bytes_accessed=2**21, transcendentals=0),
                name="product",
            )(*starts, step)
            start, product, other = lax.optimization_barrier((start, product, other))
            beside = exchange(held, 1)
            pieces = [held, beside, other, exchange(other, 1)]
            owners = [ids, tuple(d ^ 1 for d in ids), tuple(d ^ 2 for d in ids), tuple(d ^ 3 for d in ids)]
        else:
            pieces.append(other)
            owners.append(tuple(d ^ distance for d in ids))
        distance //= 2

    table = symbol_table(order)
    early = pl.pallas_call(
        symbol_kernel,
        out_shape=jax.ShapeDtypeStruct((sum(piece.shape[0] for piece in pieces[:-1]), 2 * width), jnp.float32),
        in_specs=[SMEM] + [VMEM] * len(pieces),
        out_specs=VMEM,
        compiler_params=limit,
        cost_estimate=pl.CostEstimate(flops=10**9, bytes_accessed=2**21, transcendentals=0),
        name="symbol",
    )(materials, *pieces[:-1], table)
    early, last = lax.optimization_barrier((early, pieces[-1]))
    half = [pltpu.VMEM((total, width), jnp.bfloat16)]
    result = pl.pallas_call(
        functools.partial(apply_kernel, owners),
        out_shape=jax.ShapeDtypeStruct(by_order.shape, jnp.float32),
        in_specs=[SMEM] + [VMEM] * 8,
        out_specs=pl.BlockSpec(memory_space=pl.ANY),
        scratch_shapes=[
            pltpu.VMEM((lines, 2 * width), jnp.float32),
            pltpu.VMEM((total, width), jnp.float32),
            pltpu.VMEM(by_order.shape, jnp.float32),
            pltpu.SemaphoreType.DMA((columns,)),
        ]
        + half * 4,
        compiler_params=pltpu.CompilerParams(vmem_limit_bytes=10 * 2**20),
        cost_estimate=pl.CostEstimate(flops=1000000000, bytes_accessed=4194304, transcendentals=0),
        name="apply",
    )(
        materials,
        start,
        product,
        early,
        last,
        table,
        np.concatenate([step, back]),
        inverse,
        to_orders,
    )
    return jnp.swapaxes(result, 1, 2)


def solution(mesh):
    in_specs = (P(("grp", "long"), None), P("grp"), P(("grp", "long"), None, None, None))
    out_specs = P(("grp", "long"), None, None, None)
    return jax.shard_map(local, mesh=mesh, in_specs=in_specs, out_specs=out_specs, check_vma=False)
```

```python
import functools
import math

import jax
import jax.numpy as jnp
import numpy as np
from jax import lax
from jax.experimental import pallas as pl
from jax.experimental.pallas import tpu as pltpu
from jax.sharding import PartitionSpec as P

NMAT = 4
NS_ITERS = 3
LANES = 128
BLOCK = 128


def up(value, step):
    return -(-value // step) * step


def split(x):
    high = x.astype(jnp.bfloat16)
    low = (x - high.astype(jnp.float32)).astype(jnp.bfloat16)
    return high, low


def dot(a, b):
    return jnp.dot(a, b, preferred_element_type=jnp.float32)


def dot_split(a, b):
    return dot(a[0], b[0]) + dot(a[1], b[0]) + dot(a[0], b[1])


def split_table(table):
    table = np.asarray(table, np.float32)
    high = table.astype(jnp.bfloat16)
    low = (table - high.astype(np.float32)).astype(jnp.bfloat16)
    return np.stack([high, low])


def turn(product, period):
    return np.mod(product, period) * (2.0 * math.pi / period)


def pixel_tables(npix, order):
    width = up(order, LANES)
    k = np.arange(order)
    inner = np.zeros((LANES, 2 * width))
    angle = turn(np.arange(LANES)[:, None] * k[None, :], npix)
    inner[:, :order] = np.cos(angle) / npix
    inner[:, width : width + order] = np.sin(angle) / npix
    chunks = npix // LANES
    outer = np.zeros((chunks, 2 * width), np.float32)
    angle = turn(LANES * np.arange(chunks)[:, None] * k[None, :], npix)
    outer[:, :order] = np.cos(angle)
    outer[:, width : width + order] = np.sin(angle)
    return split_table(inner), outer


def symbol_table(order):
    width = up(order, LANES)
    k = np.arange(order)
    weight = np.where(k == 0, 1.0, 2.0)[:, None]
    table = np.zeros((2 * width, 2 * width))
    for half in range(2):
        angle = turn(k[:, None] * (2 * np.arange(order)[None, :] + half), 2 * order)
        columns = slice(half * width, half * width + order)
        table[:order, columns] = weight * np.cos(angle)
        table[width : width + order, columns] = weight * np.sin(angle)
    return split_table(table)


def order_tables(order, scale):
    width = up(order, LANES)
    centred = np.arange(order) - (order - 1) // 2
    whole = 2 * np.arange(order)
    angle = turn(centred[:, None] * whole[None, :], 2 * order)
    forward = np.zeros((width, 2 * width))
    forward[:order, :order] = np.cos(angle)
    forward[:order, width : width + order] = np.sin(angle)
    inverse = np.zeros((width, 2 * width))
    inverse[:order, :order] = np.cos(angle).T * (scale / order)
    inverse[:order, width : width + order] = np.sin(angle).T * (scale / order)
    gap = whole[:, None] - (whole + 1)[None, :]
    angle = turn(centred[:, None, None] * gap[None], 2 * order)
    step = np.zeros((width, width))
    step[:order, :order] = np.cos(angle).sum(0) / order
    return split_table(forward), split_table(inverse), split_table(step), split_table(step.T)


def line_tables(lines, yord, rows, kept):
    half = (yord - 1) // 2
    angle = turn(np.arange(lines)[:, None] * (np.arange(kept) - half)[None, :], lines)
    cosine, sine = np.zeros((lines, rows)), np.zeros((lines, rows))
    cosine[:, :kept], sine[:, :kept] = np.cos(angle), np.sin(angle)
    spread = np.block([[cosine, -sine], [sine, cosine]])
    return split_table(spread), split_table(spread.T)


def scale_of(materials):
    low = functools.reduce(jnp.minimum, materials)
    high = functools.reduce(jnp.maximum, materials)
    full = lambda value: jnp.full((1, LANES), value, jnp.float32)
    return 2.0 / (1.0 / full(low) + 1.0 / full(high))


def coefficient_kernel(mats, pixels, inner, outer, out):
    inverse = [1.0 / jnp.full((1, LANES), mats[i], jnp.float32) for i in range(NMAT)]
    lines, npix = pixels.shape
    width = outer.shape[1] // 2
    chunks = npix // LANES
    parts = []
    for chunk in range(chunks):
        index = pixels[:, chunk * LANES : (chunk + 1) * LANES]
        value = jnp.zeros((lines, LANES), jnp.float32)
        for i in range(NMAT):
            value = value + jnp.where(index == i, inverse[i], 0.0)
        parts.append(value)
    inside = dot_split(split(jnp.concatenate(parts, 0)), (inner[0], inner[1]))
    real = jnp.zeros((lines, width), jnp.float32)
    imag = jnp.zeros((lines, width), jnp.float32)
    for chunk in range(chunks):
        rows = slice(chunk * lines, (chunk + 1) * lines)
        in_cos, in_sin = inside[rows, :width], inside[rows, width:]
        out_cos, out_sin = outer[chunk : chunk + 1, :width], outer[chunk : chunk + 1, width:]
        real = real + in_cos * out_cos - in_sin * out_sin
        imag = imag - in_cos * out_sin - in_sin * out_cos
    out[:, :width] = real
    out[:, width:] = imag


def pair(ref):
    return ref[0], ref[1]


def spread_kernel(panel, forward, to_lines, out, folded):
    _, yord, _, order = panel.shape
    width = out.shape[1]
    rows = folded.shape[1] // 2
    double_lines = to_lines.shape[1]
    lines = double_lines // 2
    kept = min(lines, yord)
    for c in range(folded.shape[0]):
        folded[c] = jnp.zeros((2 * rows, width), jnp.float32)
        for part in range(2):
            base = part * rows
            folded[c, base : base + kept, :order] = panel[c, :kept, part, :]
            for first in range(lines, yord, lines):
                count = min(lines, yord - first)
                folded[c, base : base + count, :order] += panel[c, first : first + count, part, :]
        both = dot_split(split(folded[c]), pair(forward))
        cosine, sine = both[:, :width], both[:, width:]
        real = cosine[:rows] + sine[rows:]
        imag = cosine[rows:] - sine[:rows]
        high, low = split(jnp.concatenate([real, imag], 0))
        value = dot(to_lines[0], high) + dot(to_lines[1], high) + dot(to_lines[0], low)
        out[c * double_lines : (c + 1) * double_lines, :] = value


def sweeps(count, half, start_of, first_of, symbol, steps, state, now, other, sums):
    lines, width = symbol.shape[0], state.shape[1]
    blocks = half // BLOCK
    per_section = blocks // 2

    def rows(unit, block):
        return slice(unit * half + block * BLOCK, unit * half + (block + 1) * BLOCK)

    def symbol_rows(unit, block, part):
        first = (unit * half + block * BLOCK) % lines
        return symbol[first : first + BLOCK, part * width : (part + 1) * width]

    def issue(stage, section):
        high, low = now if stage == 0 else other
        own = range(section * per_section, (section + 1) * per_section)
        for unit in range(2):
            for part in range(2):
                pltpu.matmul_push_rhs(steps[2 * stage + part], part, unit)
        for block in own:
            for unit in range(2):
                load = 0 if block == own[0] else None
                pltpu.matmul_acc_lhs(sums[unit * blocks + block], high[rows(unit, block)], load_staged_rhs=load)
                pltpu.matmul_acc_lhs(sums[unit * blocks + block], low[rows(unit, block)])
        for block in own:
            for unit in range(2):
                load = 1 if block == own[0] else None
                pltpu.matmul_acc_lhs(sums[unit * blocks + block], high[rows(unit, block)], load_staged_rhs=load)

    def first_product(section):
        for block in range(section * per_section, (section + 1) * per_section):
            for unit in range(2):
                place = rows(unit, block)
                other[0][place], other[1][place] = split(first_of(unit, block) * symbol_rows(unit, block, 1))
                state[place] = start_of(unit, block)

    def finish(stage, section):
        for block in range(section * per_section, (section + 1) * per_section):
            for unit in range(2):
                place = rows(unit, block)
                value = pltpu.matmul_pop(sums[unit * blocks + block])
                if stage == 0:
                    high, low = split(value * symbol_rows(unit, block, 1))
                    other[0][place], other[1][place] = high, low
                else:
                    value = start_of(unit, block) + state[place] * symbol_rows(unit, block, 0) + value
                    state[place] = value
                    now[0][place], now[1][place] = split(value)

    def body(_, carry):
        issue(0, 0)
        finish(1, 1)
        issue(0, 1)
        finish(0, 0)
        issue(1, 0)
        finish(0, 1)
        issue(1, 1)
        finish(1, 0)
        return carry

    for section in range(2):
        first_product(section)
        issue(1, section)
    finish(1, 0)
    lax.fori_loop(0, count - 1, body, 0)
    finish(1, 1)


def symbol_kernel(mats, *refs):
    pieces, table, out = refs[:-2], refs[-2], refs[-1]
    factor = scale_of([mats[i] for i in range(NMAT)])[0, 0]
    values = jnp.concatenate([piece[...] for piece in pieces], 0)
    out[...] = 0.5 - (0.5 * factor) * dot_split(split(values), pair(table))


def product_kernel(*refs):
    sources, step, both, out = refs[:-3], refs[-3], refs[-2], refs[-1]
    rows = sources[0].shape[0]
    for i, source in enumerate(sources):
        for first in range(0, rows, 2 * BLOCK):
            place = slice(first, first + 2 * BLOCK)
            value = source[place, :]
            target = slice(i * rows + first, i * rows + first + 2 * BLOCK)
            both[target, :] = value
            out[target, :] = dot_split(split(value), pair(step))


def unit_issue(lhs, rhs, unit, sums):
    depth = lhs[0].shape[1]
    tile = sums.shape[1]
    for first in range(0, depth, tile):
        inner = slice(first, first + tile)
        for part in range(2):
            pltpu.matmul_push_rhs(rhs[part][inner], part, unit)
        pltpu.matmul_acc_lhs(sums, lhs[0][:, inner], load_staged_rhs=0)
        pltpu.matmul_acc_lhs(sums, lhs[1][:, inner])
        pltpu.matmul_acc_lhs(sums, lhs[0][:, inner], load_staged_rhs=1)


def unit_product(lhs, rhs, unit, sums):
    unit_issue(lhs, rhs, unit, sums)
    return pltpu.matmul_pop(sums)


def apply_kernel(owners, mats, start, product, early, last, *refs):
    me = lax.axis_index("long")
    table, steps, inverse, to_orders, out, symbol, state, result, ready, *splits = refs
    now, other = splits[:2], splits[2:]
    columns, yord, _, order = out.shape
    lines = symbol.shape[0]
    width = state.shape[1]
    rows = to_orders.shape[1] // 2
    half = state.shape[0] // 2
    factor = scale_of([mats[i] for i in range(NMAT)])[0, 0]

    def place_of(distance, own):
        return pl.ds(pl.multiple_of((me ^ distance) * own, own), own)

    own = last.shape[0] // len(owners[-1])
    values = split(last[...])

    def last_symbols(*sums):
        for unit in range(2):
            columns_of = slice(unit * width, (unit + 1) * width)
            value = unit_product(values, (table.at[0, :, columns_of], table.at[1, :, columns_of]), unit, sums[unit])
            value = 0.5 - (0.5 * factor) * value
            for index, distance in enumerate(owners[-1]):
                symbol[place_of(distance, own), columns_of] = value[index * own : (index + 1) * own]

    for index, distance in enumerate(d for ids in owners[:-1] for d in ids):
        symbol[place_of(distance, own), :] = early[index * own : (index + 1) * own, :]
    pl.run_scoped(last_symbols, *[pltpu.ACC(unit)((last.shape[0], width), jnp.float32) for unit in range(2)])

    def start_of(unit, block):
        first = unit * half + block * BLOCK
        return start[first : first + BLOCK]

    def first_of(unit, block):
        first = unit * half + block * BLOCK
        return product[first : first + BLOCK]

    def run(*sums):
        sweeps(2**NS_ITERS - 1, half, start_of, first_of, symbol, steps, state, now, other, sums)

    pl.run_scoped(run, *[pltpu.ACC(unit)((BLOCK, width), jnp.float32) for unit in range(2) for _ in range(half // BLOCK)])

    def copy_out(c):
        return pltpu.make_async_copy(result.at[c], out.at[c], ready.at[c])

    unit_of = [c * 2 * lines // half if columns > 1 else 0 for c in range(columns)]
    order_of = sorted(range(columns), key=lambda c: (c % max(columns // 2, 1), c))
    buffers = min(2, columns)

    def all_columns(*sums):
        in_orders, in_panel = sums[:columns], sums[columns:]

        def transform(index):
            c = order_of[index]
            value = split(pltpu.matmul_pop(in_orders[c]) * factor)
            for side in range(2):
                table_of = tuple(inverse.at[part, :, side * width : (side + 1) * width] for part in range(2))
                unit_issue(value, table_of, side, in_panel[2 * (index % buffers) + side])

        def leave(index):
            c = order_of[index]
            cosine, sine = (pltpu.matmul_pop(in_panel[2 * (index % buffers) + side]) for side in range(2))
            real = cosine[:rows] - sine[rows:]
            imag = cosine[rows:] + sine[:rows]
            for part, value in enumerate((real, imag)):
                for first in range(0, yord, lines):
                    count = min(lines, yord - first)
                    result[c, first : first + count, part, :] = value[:count, :order]
            copy_out(c).start()

        for c in order_of:
            place = slice(c * 2 * lines, (c + 1) * 2 * lines)
            unit_issue((to_orders[0], to_orders[1]), (now[0].at[place], now[1].at[place]), unit_of[c], in_orders[c])
        for index in range(columns):
            transform(index)
            if index + 1 >= buffers:
                leave(index + 1 - buffers)
        for index in range(columns + 1 - buffers, columns):
            leave(index)

    column_sums = [pltpu.ACC(unit)((2 * rows, width), jnp.float32) for unit in unit_of]
    panel_sums = [pltpu.ACC(i % 2)((2 * rows, width), jnp.float32) for i in range(2 * buffers)]
    pl.run_scoped(all_columns, *column_sums, *panel_sums)
    for c in range(columns):
        copy_out(c).wait()


SMEM = pl.BlockSpec(memory_space=pltpu.SMEM)
VMEM = pl.BlockSpec(memory_space=pltpu.VMEM)


def join_kernel(*refs):
    first = 0
    for piece in refs[:-1]:
        refs[-1][first : first + piece.shape[0], :] = piece[...]
        first += piece.shape[0]


def join(pieces):
    rows = sum(piece.shape[0] for piece in pieces)
    return pl.pallas_call(
        join_kernel,
        out_shape=jax.ShapeDtypeStruct((rows, pieces[0].shape[1]), jnp.float32),
        in_specs=[VMEM] * len(pieces),
        out_specs=VMEM,
        compiler_params=pltpu.CompilerParams(vmem_limit_bytes=4 * 2**20),
        cost_estimate=pl.CostEstimate(flops=0, bytes_accessed=8 * rows * pieces[0].shape[1], transcendentals=0),
        name="join",
    )(*pieces)


def local(pixel_map, materials, mode_panel):
    devices = lax.axis_size("long")
    own, npix = pixel_map.shape
    lines = own * devices
    columns, _, yord, order = mode_panel.shape
    width = up(order, LANES)
    kept = min(lines, yord)
    rows = up(kept, 16)
    groups = 2 if columns % 2 == 0 else 1
    share = columns // groups
    total = columns * 2 * lines
    limit = pltpu.CompilerParams(vmem_limit_bytes=4 * 2**20)

    inner, outer = pixel_tables(npix, order)
    mine = pl.pallas_call(
        coefficient_kernel,
        out_shape=jax.ShapeDtypeStruct((own, 2 * width), jnp.float32),
        in_specs=[SMEM] + [VMEM] * 3,
        out_specs=VMEM,
        compiler_params=pltpu.CompilerParams(vmem_limit_bytes=56 * 2**20),
        cost_estimate=pl.CostEstimate(flops=3 * 10**9, bytes_accessed=2**22, transcendentals=0),
        name="coefficient",
    )(materials, pixel_map, inner, outer)

    forward, inverse, step, back = order_tables(order, 1.0 / lines)
    to_lines, to_orders = line_tables(lines, yord, rows, kept)

    def exchange(block, distance):
        return lax.ppermute(block, "long", [(i, i ^ distance) for i in range(devices)])

    by_order = jnp.swapaxes(mode_panel, 1, 2)
    pieces, owners, starts = [mine], [(0,)], []
    distance = devices // 2
    while distance > 1:
        held = join(pieces) if len(pieces) > 1 else mine
        ids = tuple(d for piece in owners for d in piece)
        other = exchange(held, distance)
        if len(starts) < groups:
            group = len(starts)
            start = pl.pallas_call(
                spread_kernel,
                grid=(1,),
                out_shape=jax.ShapeDtypeStruct((share * 2 * lines, width), jnp.float32),
                in_specs=[pl.BlockSpec((share, yord, 2, order), lambda _, group=group: (group, 0, 0, 0)), VMEM, VMEM],
                out_specs=VMEM,
                scratch_shapes=[pltpu.VMEM((share, 2 * rows, width), jnp.float32)],
                compiler_params=limit,
                cost_estimate=pl.CostEstimate(flops=10**9, bytes_accessed=2**21, transcendentals=0),
                name="spread",
            )(by_order, forward, to_lines)
            start, other = lax.optimization_barrier((start, other))
            starts.append(start)
        if distance == 2:
            start, product = pl.pallas_call(
                product_kernel,
                out_shape=[jax.ShapeDtypeStruct((total, width), jnp.float32)] * 2,
                in_specs=[VMEM] * (groups + 1),
                out_specs=[VMEM] * 2,
                compiler_params=limit,
                cost_estimate=pl.CostEstimate(flops=10**9, bytes_accessed=2**21, transcendentals=0),
                name="product",
            )(*starts, step)
            start, product, late = lax.optimization_barrier((start, product, held))
            product, other = lax.optimization_barrier((product, other))
            beside = exchange(late, 1)
            pieces = [held, beside, other, exchange(other, 1)]
            owners = [ids, tuple(d ^ 1 for d in ids), tuple(d ^ 2 for d in ids), tuple(d ^ 3 for d in ids)]
        else:
            pieces.append(other)
            owners.append(tuple(d ^ distance for d in ids))
        distance //= 2

    table = symbol_table(order)
    early = pl.pallas_call(
        symbol_kernel,
        out_shape=jax.ShapeDtypeStruct((sum(piece.shape[0] for piece in pieces[:-1]), 2 * width), jnp.float32),
        in_specs=[SMEM] + [VMEM] * len(pieces),
        out_specs=VMEM,
        compiler_params=limit,
        cost_estimate=pl.CostEstimate(flops=10**9, bytes_accessed=2**21, transcendentals=0),
        name="symbol",
    )(materials, *pieces[:-1], table)
    early, last = lax.optimization_barrier((early, pieces[-1]))
    half = [pltpu.VMEM((total, width), jnp.bfloat16)]
    result = pl.pallas_call(
        functools.partial(apply_kernel, owners),
        out_shape=jax.ShapeDtypeStruct(by_order.shape, jnp.float32),
        in_specs=[SMEM] + [VMEM] * 8,
        out_specs=pl.BlockSpec(memory_space=pl.ANY),
        scratch_shapes=[
            pltpu.VMEM((lines, 2 * width), jnp.float32),
            pltpu.VMEM((total, width), jnp.float32),
            pltpu.VMEM(by_order.shape, jnp.float32),
            pltpu.SemaphoreType.DMA((columns,)),
        ]
        + half * 4,
        compiler_params=pltpu.CompilerParams(vmem_limit_bytes=10 * 2**20),
        cost_estimate=pl.CostEstimate(flops=1000000000, bytes_accessed=4194304, transcendentals=0),
        name="apply",
    )(
        materials,
        start,
        product,
        early,
        last,
        table,
        np.concatenate([step, back]),
        inverse,
        to_orders,
    )
    return jnp.swapaxes(result, 1, 2)


def solution(mesh):
    in_specs = (P(("grp", "long"), None), P("grp"), P(("grp", "long"), None, None, None))
    out_specs = P(("grp", "long"), None, None, None)
    return jax.shard_map(local, mesh=mesh, in_specs=in_specs, out_specs=out_specs, check_vma=False)
```
